32 devices in a mesh: band: 2 (over x), dx: 4 (over y, core), dy: 4 (over z).
Axes of the slice: x: 2, y: 2, z: 4, core: 2. Of those that a mesh axis runs over, the one named last changes fastest.
Arguments:
- orbitals: float32 [4, 128, 128, 128], P('band', 'dx', 'dy'), may hold values from -6 to 6
- occupations: float32 [4], P('band'), may hold values from 0.02 to 0.2
- core_density: float32 [128, 128, 128], P('dx', 'dy', 'band'), may hold values from 0.5 to 5
- external: float32 [128, 128, 128], P('dx', 'dy', 'band'), may hold values from -2 to 0
Outputs:
- applied: float32 [4, 128, 128, 128], P('band', 'dx', 'dy')
- potential: float32 [128, 128, 128], P('dx', 'dy', 'band')
The draws below stay inside these ranges and needn't reach their ends.
All inputs are finite; a program needn't handle non-finite values.
Results may differ from the reference program's by a relative error of at most 0.0001.
Values sent between devices are 32-bit elements; how exact they have to be, the bound alone decides.
No kernel may reach another device: no remote copies, remote signals or barrier semaphores. Data moves between devices by JAX's collectives and lax.ppermute only.
A program may use at most 128 MiB of HBM per device.

```python
import math
import jax
import jax.numpy as jnp
from jax import lax

NB = 2
NZ = 128
BANDS = 4
NX = 128
NY = 128


def strengthened(entries, stream_key, source, target, blocks, factor):
    owner, partner = [(jnp.arange(entries.shape[position]) // (entries.shape[position] // blocks)).reshape([-1 if axis == position else 1 for axis in range(entries.ndim)]) for position in (source, target)]
    chosen = jax.random.permutation(stream_key, blocks)[partner]
    strong = (owner == chosen) | (owner == (partner + blocks // 2) % blocks)
    return jnp.where(strong, factor * entries, entries)


def steps_of(rng, extent, shards, low, high):
    factor_of, own = 1.0, jax.random.fold_in(rng, 6)
    for dim, parts in shards:
        steps = jnp.exp(jax.random.uniform(jax.random.fold_in(own, dim), (parts,), jnp.float32, low / len(shards), high / len(shards)))
        factor_of = factor_of * jnp.repeat(steps, extent[dim] // parts).reshape([-1 if axis == dim else 1 for axis in range(len(extent))])
    return factor_of


def heavy_noise(own_key, shape, spread, reach, shards, heavy, held_as=jnp.bfloat16):
    entries = spread * jax.random.normal(own_key, shape, jnp.float32)
    if shards:
        entries = entries * steps_of(own_key, shape, shards, -0.22, 0.18)
    return jnp.clip(strengthened(entries, jax.random.fold_in(own_key, 3), *heavy), -reach, reach).astype(held_as)


def setup_inputs(seed: int = 0) -> dict:
    arg_keys = jax.random.split(jax.random.key(seed), 5)
    return {
        "orbitals": heavy_noise(arg_keys[0], (BANDS, NX, NY, NZ), 1.0, 6.0, ((0, 2), (1, 4), (2, 4)), (0, 3, 2, 2.0), jnp.float32),
        "occupations": jnp.clip(jnp.exp(math.log(0.2) - 2.3025851 * jax.random.uniform(arg_keys[1], (BANDS,), jnp.float32) ** steps_of(arg_keys[1], (BANDS,), ((0, 2),), -0.2, 0.2)), 0.02, 0.2),
        "core_density": jnp.clip(jnp.exp(math.log(5.0) - 2.3025851 * jax.random.uniform(arg_keys[2], (NX, NY, NZ), jnp.float32) ** steps_of(arg_keys[2], (NX, NY, NZ), ((0, 4), (1, 4), (2, 2)), -0.2, 0.2)), 0.5, 5.0),
        "external": jnp.clip(-2.0 + 2.0 * jax.random.uniform(arg_keys[3], (NX, NY, NZ), jnp.float32) ** steps_of(arg_keys[3], (NX, NY, NZ), ((0, 4), (1, 4), (2, 2)), -0.2, 0.2), -2.0, 0.0),
    }


coeffs = (-5369.0 / 1800.0, 12.0 / 7.0, -15.0 / 56.0, 10.0 / 189.0, -1.0 / 112.0, 2.0 / 1925.0, -1.0 / 16632.0)
grid_step = 2.0
slater = (3.0 / math.pi) ** (1.0 / 3.0)


def laplace(field):
    summed = 3.0 * coeffs[0] * field
    for dimension in range(3):
        for offset in range(1, 7):
            summed = summed + coeffs[offset] * (jnp.roll(field, offset, dimension) + jnp.roll(field, -offset, dimension))
    return summed / (grid_step * grid_step)


def reference(orbitals, occupations, core_density, external):
    blocks = orbitals.reshape(BANDS // NB, NB, NX, NY, NZ)
    weights = occupations.reshape(BANDS // NB, NB)

    def add_block(carry, pair):
        block, weight = pair
        return carry + jnp.sum(weight[:, None, None, None] * block * block, axis=0), None

    start = jnp.zeros((NX, NY, NZ), jnp.float32)
    summed, unused = lax.scan(add_block, start, (blocks, weights))
    density = summed + core_density
    potential = external - slater * density ** (1.0 / 3.0)

    def apply_block(block):
        return jax.vmap(lambda field: -0.5 * laplace(field) + potential * field)(block)

    applied = lax.map(apply_block, blocks).reshape(BANDS, NX, NY, NZ)
    return applied, potential
```

```python
import functools
import math

import jax
import jax.numpy as jnp
import numpy as np
from jax import lax
from jax.experimental import pallas as pl
from jax.experimental.pallas import tpu as pltpu
from jax.sharding import PartitionSpec as P

coeffs = (
    -5369.0 / 1800.0,
    12.0 / 7.0,
    -15.0 / 56.0,
    10.0 / 189.0,
    -1.0 / 112.0,
    2.0 / 1925.0,
    -1.0 / 16632.0,
)
reach = len(coeffs) - 1
grid_step = 2.0
slater = (3.0 / math.pi) ** (1.0 / 3.0)
scaled = tuple(-0.5 * c / (grid_step * grid_step) for c in coeffs)


def shifted(block, axis, up):
    count = lax.axis_size(axis)
    pairs = [(i, (i + 1) % count) for i in range(count)]
    if not up:
        pairs = [(target, source) for source, target in pairs]
    return lax.ppermute(block, axis, pairs)


def own_lanes(shape):
    lane = lax.broadcasted_iota(jnp.int32, shape, 1)
    return (lane < shape[1] // 2) == (lax.axis_index("band") == 0)


def halo_kernel(x_cells, y_cells, orb_ref, ylow_ref, yhigh_ref, xlow_ref, xhigh_ref):
    bands, _, z_cells = orb_ref.shape[0] // (x_cells * y_cells), None, orb_ref.shape[1]
    lines = bands * x_cells
    for i in range(reach):
        ylow_ref[i] = orb_ref[pl.ds(y_cells - reach + i, lines, stride=y_cells), :]
        yhigh_ref[i] = orb_ref[pl.ds(i, lines, stride=y_cells), :]
    for b in range(bands):
        base = b * x_cells * y_cells
        span = reach * y_cells
        xlow_ref[b] = orb_ref[pl.ds(base + x_cells * y_cells - span, span), :]
        xhigh_ref[b] = orb_ref[pl.ds(base, span), :]


def density_kernel(x_cells, y_cells, occ_ref, orb_ref, keep_ref, send_ref):
    z_cells = orb_ref.shape[1]
    bands = orb_ref.shape[0] // (x_cells * y_cells)
    own = own_lanes((y_cells, z_cells))

    def summed(x):
        total = None
        for b in range(bands):
            value = orb_ref[pl.ds((b * x_cells + x) * y_cells, y_cells), :]
            term = occ_ref[b] * value * value
            total = term if total is None else total + term
        return total

    for x in range(x_cells // 2):
        near = summed(x)
        far = pltpu.roll(summed(x + x_cells // 2), z_cells // 2, 1)
        keep_ref[x] = jnp.where(own, near, far)
        send_ref[x] = jnp.where(own, far, near)


def stencil_kernel(x_cells, y_cells, orb_ref, ymat_ref, zmat_ref, acc_ref):
    z_cells = orb_ref.shape[1]
    rows = orb_ref.shape[0]
    bands = rows // (x_cells * y_cells)
    tile = ymat_ref.shape[0]
    for start in range(0, rows, tile):
        block = orb_ref[pl.ds(start, tile), :]
        acc_ref[pl.ds(start, tile), :] = jnp.dot(
            block, zmat_ref[...], precision=lax.Precision.HIGHEST, preferred_element_type=jnp.float32
        ) + jnp.dot(
            ymat_ref[...], block, precision=lax.Precision.HIGHEST, preferred_element_type=jnp.float32
        )
    for b in range(bands):
        for y in range(0, y_cells, 8):
            column = [orb_ref[pl.ds((b * x_cells + x) * y_cells + y, 8), :] for x in range(x_cells)]
            for x in range(x_cells):
                here = pl.ds((b * x_cells + x) * y_cells + y, 8)
                total = acc_ref[here, :]
                for offset in range(1, reach + 1):
                    pair = [column[t] for t in (x - offset, x + offset) if 0 <= t < x_cells]
                    if pair:
                        total = total + scaled[offset] * sum(pair[1:], pair[0])
                acc_ref[here, :] = total


def base_kernel(keep_ref, core_ref, ext_ref, dens_ref, extp_ref):
    half = keep_ref.shape[0]
    own = lax.axis_index("band")
    for x in range(half):
        first, second = x + half * own, x + half * (1 - own)
        dens_ref[x] = keep_ref[x] + jnp.concatenate([core_ref[first], core_ref[second]], axis=1)
        extp_ref[x] = jnp.concatenate([ext_ref[first], ext_ref[second]], axis=1)


def potential_kernel(dens_ref, extp_ref, came_ref, pot_ref):
    for x in range(dens_ref.shape[0]):
        density = dens_ref[x] + came_ref[x]
        pot_ref[x] = extp_ref[x] - slater * jnp.exp(jnp.log(density) * (1.0 / 3.0))


def owned_kernel(pot_ref, out_ref):
    half, _, z_cells = pot_ref.shape
    own = lax.axis_index("band")
    for x in range(half):
        first, second = x + half * own, x + half * (1 - own)
        value = pot_ref[x]
        out_ref[first] = value[:, : z_cells // 2]
        out_ref[second] = value[:, z_cells // 2 :]


def final_kernel(
    x_cells, y_cells, packed, orb_ref, acc_ref, xlow_ref, xhigh_ref, ylow_ref, yhigh_ref, *rest
):
    out_ref = rest[-1]
    z_cells = orb_ref.shape[1]
    bands = orb_ref.shape[0] // (x_cells * y_cells)
    lines = bands * x_cells
    if packed:
        mine_ref, came_ref = rest[0], rest[1]
        own = own_lanes((y_cells, z_cells))
        half = x_cells // 2
        potential = [None] * x_cells
        for x in range(half):
            mine, came = mine_ref[x], came_ref[x]
            potential[x] = jnp.where(own, mine, came)
            potential[x + half] = pltpu.roll(jnp.where(own, came, mine), z_cells // 2, 1)
            for t in (x, x + half):
                add_plane(x_cells, y_cells, bands, t, potential[t], orb_ref, acc_ref, xlow_ref, xhigh_ref, out_ref)
    else:
        for x in range(x_cells):
            add_plane(x_cells, y_cells, bands, x, rest[0][x], orb_ref, acc_ref, xlow_ref, xhigh_ref, out_ref)
    for y in range(reach):
        low = pl.ds(y, lines, stride=y_cells)
        high = pl.ds(y_cells - 1 - y, lines, stride=y_cells)
        low_sum, high_sum = out_ref[low, :], out_ref[high, :]
        for offset in range(y + 1, reach + 1):
            low_sum = low_sum + scaled[offset] * ylow_ref[reach + y - offset]
            high_sum = high_sum + scaled[offset] * yhigh_ref[offset - 1 - y]
        out_ref[low, :] = low_sum
        out_ref[high, :] = high_sum


def add_plane(x_cells, y_cells, bands, x, potential, orb_ref, acc_ref, xlow_ref, xhigh_ref, out_ref):
    for b in range(bands):
        here = pl.ds((b * x_cells + x) * y_cells, y_cells)
        total = acc_ref[here, :] + potential * orb_ref[here, :]
        for offset in range(1, reach + 1):
            if x - offset < 0:
                row = (reach + x - offset) * y_cells
                total = total + scaled[offset] * xlow_ref[b, pl.ds(row, y_cells), :]
            if x + offset >= x_cells:
                row = (x + offset - x_cells) * y_cells
                total = total + scaled[offset] * xhigh_ref[b, pl.ds(row, y_cells), :]
        out_ref[here, :] = total


def band_matrix(size, extent, periodic):
    matrix = np.zeros((size, size), np.float32)
    for i in range(size):
        group = i // extent * extent
        for offset in range(-reach, reach + 1):
            j = i - group + offset
            if periodic:
                j %= extent
            if 0 <= j < extent:
                matrix[i, group + j] += scaled[abs(offset)]
    return matrix


def whole(count):
    return [pl.BlockSpec(memory_space=pltpu.VMEM)] * count


def call(kernel, outs, args, flops=1 << 20, scalars=0):
    shapes = [jax.ShapeDtypeStruct(shape, jnp.float32) for shape in outs]
    moved = sum(4 * math.prod(shape) for shape in outs) + sum(4 * a.size for a in args)
    return pl.pallas_call(
        kernel,
        out_shape=shapes,
        in_specs=[pl.BlockSpec(memory_space=pltpu.SMEM)] * scalars + whole(len(args) - scalars),
        out_specs=whole(len(outs)),
        cost_estimate=pl.CostEstimate(flops=flops, bytes_accessed=moved, transcendentals=0),
        compiler_params=pltpu.CompilerParams(vmem_limit_bytes=32 << 20),
    )(*args)


def on_device(orbitals, occupations, core_density, external):
    bands, x_cells, y_cells, z_cells = orbitals.shape
    rows = bands * x_cells * y_cells
    orb = orbitals.reshape(rows, z_cells)
    y_halo = (reach, bands * x_cells, z_cells)
    x_halo = (bands, reach * y_cells, z_cells)
    paired = lax.axis_size("band") == 2
    if paired:
        packed = (x_cells // 2, y_cells, z_cells)
        keep, send = call(
            functools.partial(density_kernel, x_cells, y_cells), [packed, packed], [occupations, orb], scalars=1
        )
        came = shifted(send, "band", True)
    ylow, yhigh, xlow, xhigh = call(
        functools.partial(halo_kernel, x_cells, y_cells), [y_halo, y_halo, x_halo, x_halo], [orb]
    )
    ylow, yhigh = shifted(ylow, "dy", True), shifted(yhigh, "dy", False)
    xlow, xhigh = shifted(xlow, "dx", True), shifted(xhigh, "dx", False)
    tile = 8 * y_cells
    center = band_matrix(tile, y_cells, False)
    center = center + np.float32(scaled[0]) * np.eye(tile, dtype=np.float32)
    (acc,) = call(
        functools.partial(stencil_kernel, x_cells, y_cells),
        [(rows, z_cells)],
        [orb, jnp.asarray(center), jnp.asarray(band_matrix(z_cells, z_cells, True))],
        flops=1 << 28,
    )
    if paired:
        dens, extp = call(base_kernel, [packed, packed], [keep, core_density, external])
        (mine,) = call(potential_kernel, [packed], [dens, extp, came])
        came = shifted(mine, "band", True)
        (owned,) = call(owned_kernel, [core_density.shape], [mine])
        potential = [mine, came]
    else:
        own_density = jnp.sum(occupations[:, None, None, None] * orbitals * orbitals, axis=0)
        shared = lax.psum_scatter(own_density, "band", scatter_dimension=2, tiled=True)
        owned = external - slater * (shared + core_density) ** (1.0 / 3.0)
        potential = [lax.all_gather(owned, "band", axis=2, tiled=True)]
    (applied,) = call(
        functools.partial(final_kernel, x_cells, y_cells, paired),
        [(rows, z_cells)],
        [orb, acc, xlow, xhigh, ylow, yhigh, *potential],
    )
    return applied.reshape(orbitals.shape), owned


def solution(mesh):
    return jax.shard_map(
        on_device,
        mesh=mesh,
        in_specs=(
            P("band", "dx", "dy", None),
            P("band"),
            P("dx", "dy", "band"),
            P("dx", "dy", "band"),
        ),
        out_specs=(P("band", "dx", "dy", None), P("dx", "dy", "band")),
        check_vma=False,
    )
```

```python
import functools
import math

import jax
import jax.numpy as jnp
import numpy as np
from jax import lax
from jax.experimental import pallas as pl
from jax.experimental.pallas import tpu as pltpu
from jax.sharding import PartitionSpec as P

coeffs = (
    -5369.0 / 1800.0,
    12.0 / 7.0,
    -15.0 / 56.0,
    10.0 / 189.0,
    -1.0 / 112.0,
    2.0 / 1925.0,
    -1.0 / 16632.0,
)
reach = len(coeffs) - 1
grid_step = 2.0
slater = (3.0 / math.pi) ** (1.0 / 3.0)
scaled = tuple(-0.5 * c / (grid_step * grid_step) for c in coeffs)


def shifted(block, axis, up):
    count = lax.axis_size(axis)
    pairs = [(i, (i + 1) % count) for i in range(count)]
    if not up:
        pairs = [(target, source) for source, target in pairs]
    return lax.ppermute(block, axis, pairs)


def own_lanes(shape):
    lane = lax.broadcasted_iota(jnp.int32, shape, 1)
    return (lane < shape[1] // 2) == (lax.axis_index("band") == 0)


def fetch_copies(x_cells, y_cells, source_ref, target_ref, sems):
    bands = source_ref.shape[0] // (x_cells * y_cells)
    quarter = x_cells // 4 * y_cells
    return [
        [
            pltpu.make_async_copy(
                source_ref.at[pl.ds((4 * b + q) * quarter, quarter), :],
                target_ref.at[pl.ds((4 * b + q) * quarter, quarter), :],
                sems.at[4 * b + q],
            )
            for b in range(bands)
            for q in (part, part + 2)
        ]
        for part in range(2)
    ]


def density_kernel(
    x_cells, y_cells, occ_ref, source_ref, orb_ref, keep_ref, send_ref, *rest
):
    *halo_refs, weight_ref, weight_sem, sems = rest
    weights = pltpu.make_async_copy(occ_ref, weight_ref, weight_sem)
    weights.start()
    copies = fetch_copies(x_cells, y_cells, source_ref, orb_ref, sems)
    for part in copies:
        for copy in part:
            copy.start()
    z_cells = orb_ref.shape[1]
    bands = orb_ref.shape[0] // (x_cells * y_cells)
    own = own_lanes((y_cells, z_cells))

    def summed(x):
        total = None
        for b in range(bands):
            value = orb_ref[pl.ds((b * x_cells + x) * y_cells, y_cells), :]
            term = weight_ref[b] * value * value
            total = term if total is None else total + term
        return total

    weights.wait()
    for part in range(2):
        for copy in copies[part]:
            copy.wait()
        for x in range(part * x_cells // 4, (part + 1) * x_cells // 4):
            near = summed(x)
            far = pltpu.roll(summed(x + x_cells // 2), z_cells // 2, 1)
            keep_ref[x] = jnp.where(own, near, far)
            send_ref[x] = jnp.where(own, far, near)
    halo_kernel(x_cells, y_cells, orb_ref, *halo_refs)


def halo_kernel(x_cells, y_cells, orb_ref, ylow_ref, yhigh_ref, xlow_ref, xhigh_ref):
    lines = orb_ref.shape[0] // y_cells
    for i in range(reach):
        ylow_ref[i] = orb_ref[pl.ds(y_cells - reach + i, lines, stride=y_cells), :]
        yhigh_ref[i] = orb_ref[pl.ds(i, lines, stride=y_cells), :]
    span, brick = reach * y_cells, x_cells * y_cells
    for b in range(lines // x_cells):
        xlow_ref[b] = orb_ref[pl.ds((b + 1) * brick - span, span), :]
        xhigh_ref[b] = orb_ref[pl.ds(b * brick, span), :]


def stencil_kernel(x_cells, y_cells, orb_ref, ymat_ref, zmat_ref, acc_ref):
    rows, z_cells = orb_ref.shape
    tile = ymat_ref.shape[1]
    for start in range(0, rows, tile):
        block = orb_ref[pl.ds(start, tile), :]
        coarse = block.astype(jnp.bfloat16)
        fine = (block - coarse.astype(jnp.float32)).astype(jnp.bfloat16)
        both = jnp.concatenate([coarse, fine], axis=1)
        along_z = jnp.dot(both, zmat_ref[...], preferred_element_type=jnp.float32)
        along_y = jnp.dot(ymat_ref[...], both, preferred_element_type=jnp.float32)
        acc_ref[pl.ds(start, tile), :] = (
            (along_z[:, :z_cells] + along_y[:tile, :z_cells])
            + (along_z[:, z_cells:] + along_y[:tile, z_cells:])
            + along_y[tile:, :z_cells]
        )
    for b in range(rows // (x_cells * y_cells)):
        for y in range(0, y_cells, 8):
            column = [orb_ref[pl.ds((b * x_cells + x) * y_cells + y, 8), :] for x in range(x_cells)]
            for x in range(x_cells):
                here = pl.ds((b * x_cells + x) * y_cells + y, 8)
                total = acc_ref[here, :]
                for offset in range(1, reach + 1):
                    pair = [column[t] for t in (x - offset, x + offset) if 0 <= t < x_cells]
                    total = total + scaled[offset] * sum(pair[1:], pair[0])
                acc_ref[here, :] = total


def base_kernel(keep_ref, core_ref, ext_ref, dens_ref, extp_ref):
    half = keep_ref.shape[0]
    own = lax.axis_index("band")
    for x in range(half):
        first, second = x + half * own, x + half * (1 - own)
        dens_ref[x] = keep_ref[x] + jnp.concatenate([core_ref[first], core_ref[second]], axis=1)
        extp_ref[x] = jnp.concatenate([ext_ref[first], ext_ref[second]], axis=1)


def potential_kernel(dens_ref, extp_ref, came_ref, pot_ref):
    for x in range(dens_ref.shape[0]):
        density = dens_ref[x] + came_ref[x]
        pot_ref[x] = extp_ref[x] - slater * jnp.exp(jnp.log(density) * (1.0 / 3.0))


def owned_kernel(pot_ref, out_ref):
    half, _, z_cells = pot_ref.shape
    own = lax.axis_index("band")
    for x in range(half):
        first, second = x + half * own, x + half * (1 - own)
        value = pot_ref[x]
        out_ref[first] = value[:, : z_cells // 2]
        out_ref[second] = value[:, z_cells // 2 :]


def border_kernel(x_cells, y_cells, inner_ref, ylow_ref, yhigh_ref, xlow_ref, xhigh_ref, acc_ref):
    lines = inner_ref.shape[0] // y_cells
    for line in range(lines):
        b, x = divmod(line, x_cells)
        if reach <= x < x_cells - reach:
            continue
        here = pl.ds(line * y_cells, y_cells)
        total = inner_ref[here, :]
        for offset in range(1, reach + 1):
            if x - offset < 0:
                row = (reach + x - offset) * y_cells
                total = total + scaled[offset] * xlow_ref[b, pl.ds(row, y_cells), :]
            if x + offset >= x_cells:
                row = (x + offset - x_cells) * y_cells
                total = total + scaled[offset] * xhigh_ref[b, pl.ds(row, y_cells), :]
        acc_ref[here, :] = total
    for y in range(reach):
        low = pl.ds(y, lines, stride=y_cells)
        high = pl.ds(y_cells - 1 - y, lines, stride=y_cells)
        low_sum, high_sum = acc_ref[low, :], acc_ref[high, :]
        for offset in range(y + 1, reach + 1):
            low_sum = low_sum + scaled[offset] * ylow_ref[reach + y - offset]
            high_sum = high_sum + scaled[offset] * yhigh_ref[offset - 1 - y]
        acc_ref[low, :] = low_sum
        acc_ref[high, :] = high_sum


def final_kernel(x_cells, y_cells, orb_ref, acc_ref, mine_ref, came_ref, out_ref, held_ref, sems):
    z_cells = orb_ref.shape[1]
    bands = orb_ref.shape[0] // (x_cells * y_cells)
    own = own_lanes((y_cells, z_cells))
    half, part = x_cells // 2, x_cells // 8
    copies = []
    for x in range(half):
        mine, came = mine_ref[x], came_ref[x]
        near = jnp.where(own, mine, came)
        far = pltpu.roll(jnp.where(own, came, mine), z_cells // 2, 1)
        for t, potential in ((x, near), (x + half, far)):
            for b in range(bands):
                here = pl.ds((b * x_cells + t) * y_cells, y_cells)
                held_ref[here, :] = acc_ref[here, :] + potential * orb_ref[here, :]
        if x % part == part - 1:
            for first in (x + 1 - part, x + 1 - part + half):
                for b in range(bands):
                    piece = pl.ds((b * x_cells + first) * y_cells, part * y_cells)
                    copy = pltpu.make_async_copy(
                        held_ref.at[piece, :], out_ref.at[piece, :], sems.at[len(copies)]
                    )
                    copy.start()
                    copies.append(copy)
    for copy in copies:
        copy.wait()


def whole_kernel(orb_ref, acc_ref, potential_ref, out_ref):
    planes, y_cells, _ = potential_ref.shape
    for line in range(orb_ref.shape[0] // y_cells):
        here = pl.ds(line * y_cells, y_cells)
        out_ref[here, :] = acc_ref[here, :] + potential_ref[line % planes] * orb_ref[here, :]


def band_matrix(size, extent, periodic):
    matrix = np.zeros((size, size), np.float32)
    for i in range(size):
        group = i // extent * extent
        for offset in range(-reach, reach + 1):
            j = i - group + offset
            if periodic:
                j %= extent
            if 0 <= j < extent:
                matrix[i, group + j] += scaled[abs(offset)]
    return matrix


def split_constant(matrix):
    coarse = matrix.astype(jnp.bfloat16)
    return coarse, (matrix - coarse.astype(np.float32)).astype(jnp.bfloat16)


def call(kernel, outs, args, spaces=None, out_spaces=None, scratch=(), flops=1 << 20, aliases=None):
    shapes = [jax.ShapeDtypeStruct(shape, jnp.float32) for shape in outs]
    moved = sum(4 * math.prod(shape) for shape in outs) + sum(4 * a.size for a in args)
    spaces = spaces or [pltpu.VMEM] * len(args)
    out_spaces = out_spaces or [pltpu.VMEM] * len(outs)
    return pl.pallas_call(
        kernel,
        out_shape=shapes,
        in_specs=[pl.BlockSpec(memory_space=space) for space in spaces],
        out_specs=[pl.BlockSpec(memory_space=space) for space in out_spaces],
        scratch_shapes=list(scratch),
        input_output_aliases=aliases or {},
        cost_estimate=pl.CostEstimate(flops=flops, bytes_accessed=moved, transcendentals=0),
        compiler_params=pltpu.CompilerParams(vmem_limit_bytes=16 << 20),
    )(*args)


def on_device(orbitals, occupations, core_density, external):
    bands, x_cells, y_cells, z_cells = orbitals.shape
    rows = bands * x_cells * y_cells
    orb = pltpu.with_memory_space_constraint(orbitals.reshape(rows, z_cells), pltpu.HBM)
    flat = (rows, z_cells)
    y_halo = (reach, bands * x_cells, z_cells)
    x_halo = (bands, reach * y_cells, z_cells)
    bind = lambda kernel: functools.partial(kernel, x_cells, y_cells)
    paired = lax.axis_size("band") == 2
    if paired:
        packed = (x_cells // 2, y_cells, z_cells)
        orb, keep, send, *halos = call(
            bind(density_kernel),
            [flat, packed, packed, y_halo, y_halo, x_halo, x_halo],
            [pltpu.with_memory_space_constraint(occupations, pltpu.HBM), orb],
            spaces=[pltpu.HBM, pltpu.HBM],
            scratch=[
                pltpu.SMEM(occupations.shape, jnp.float32),
                pltpu.SemaphoreType.DMA,
                pltpu.SemaphoreType.DMA((4 * bands,)),
            ],
        )
        came = shifted(send, "band", True)
    else:
        halos = call(bind(halo_kernel), [y_halo, y_halo, x_halo, x_halo], [orb])
    ylow, yhigh, xlow, xhigh = halos
    xlow, xhigh = shifted(xlow, "dx", True), shifted(xhigh, "dx", False)
    ylow, yhigh = shifted(ylow, "dy", True), shifted(yhigh, "dy", False)
    tile = 8 * y_cells
    middle = np.float32(scaled[0]) * np.eye(tile, dtype=np.float32)
    coarse, fine = split_constant(band_matrix(tile, y_cells, False) + middle)
    ymat = np.concatenate([coarse, fine], axis=0)
    coarse, fine = split_constant(band_matrix(z_cells, z_cells, True))
    zmat = np.block([[coarse, fine], [coarse, np.zeros_like(fine)]])
    (acc,) = call(
        bind(stencil_kernel), [flat], [orb, jnp.asarray(ymat), jnp.asarray(zmat)], flops=1 << 28
    )
    if paired:
        dens, extp = call(base_kernel, [packed, packed], [keep, core_density, external])
        dens, acc = lax.optimization_barrier((dens, acc))
        (mine,) = call(potential_kernel, [packed], [dens, extp, came])
        came = shifted(mine, "band", True)
        (owned,) = call(owned_kernel, [core_density.shape], [mine])
    else:
        own_density = jnp.sum(occupations[:, None, None, None] * orbitals * orbitals, axis=0)
        shared = lax.psum_scatter(own_density, "band", scatter_dimension=2, tiled=True)
        owned = external - slater * (shared + core_density) ** (1.0 / 3.0)
        potential = lax.all_gather(owned, "band", axis=2, tiled=True)
    (acc,) = call(bind(border_kernel), [flat], [acc, ylow, yhigh, xlow, xhigh], aliases={0: 0}, flops=1 << 34)
    if paired:
        (applied,) = call(
            bind(final_kernel),
            [flat],
            [orb, acc, mine, came],
            out_spaces=[pltpu.HBM],
            scratch=[pltpu.VMEM(flat, jnp.float32), pltpu.SemaphoreType.DMA((8 * bands,))],
        )
    else:
        (applied,) = call(whole_kernel, [flat], [orb, acc, potential])
    return applied.reshape(orbitals.shape), owned


def solution(mesh):
    return jax.shard_map(
        on_device,
        mesh=mesh,
        in_specs=(
            P("band", "dx", "dy", None),
            P("band"),
            P("dx", "dy", "band"),
            P("dx", "dy", "band"),
        ),
        out_specs=(P("band", "dx", "dy", None), P("dx", "dy", "band")),
        check_vma=False,
    )
```

```python
import functools
import math

import jax
import jax.numpy as jnp
import numpy as np
from jax import lax
from jax.experimental import pallas as pl
from jax.experimental.pallas import tpu as pltpu
from jax.sharding import PartitionSpec as P

coeffs = (
    -5369.0 / 1800.0,
    12.0 / 7.0,
    -15.0 / 56.0,
    10.0 / 189.0,
    -1.0 / 112.0,
    2.0 / 1925.0,
    -1.0 / 16632.0,
)
reach = len(coeffs) - 1
FY, FX, FM = 0, 1 << 32, 0
grid_step = 2.0
slater = (3.0 / math.pi) ** (1.0 / 3.0)
scaled = tuple(-0.5 * c / (grid_step * grid_step) for c in coeffs)


def exchanged(block, axis, first):
    count = lax.axis_size(axis)
    pairs = [((first + i) % count, (first + (i ^ 1)) % count) for i in range(count)]
    return lax.ppermute(block, axis, pairs)


def own_lanes(shape):
    lane = lax.broadcasted_iota(jnp.int32, shape, 1)
    return (lane < shape[1] // 2) == (lax.axis_index("band") == 0)


def density_kernel(
    x_cells, y_cells, occ_ref, source_ref, orb_ref, keep_ref, send_ref, extra_ref, weight_ref, weight_sem, sems
):
    rows, z_cells = orb_ref.shape
    bands, half = rows // (x_cells * y_cells), x_cells // 2
    group = half // 4
    weights = pltpu.make_async_copy(occ_ref, weight_ref, weight_sem)
    weights.start()
    copies = []
    for part in range(4):
        for b in range(bands):
            for first in (part * group, part * group + half):
                piece = pl.ds((b * x_cells + first) * y_cells, group * y_cells)
                copies.append(
                    pltpu.make_async_copy(source_ref.at[piece, :], orb_ref.at[piece, :], sems.at[len(copies)])
                )
                copies[-1].start()
    own = own_lanes((y_cells, z_cells))

    def summed(x):
        total = None
        for b in range(bands):
            value = orb_ref[pl.ds((b * x_cells + x) * y_cells, y_cells), :]
            term = weight_ref[b] * value * value
            total = term if total is None else total + term
        return total

    weights.wait()
    late = send_ref.shape[0]
    for part in range(4):
        for copy in copies[2 * bands * part : 2 * bands * (part + 1)]:
            copy.wait()
        for x in range(part * group, (part + 1) * group):
            near = summed(x)
            far = pltpu.roll(summed(x + half), z_cells // 2, 1)
            keep_ref[x] = jnp.where(own, near, far)
            other = jnp.where(own, far, near)
            if x < late:
                send_ref[x] = other
            else:
                extra_ref[x - late] = other


def halo_kernel(x_cells, y_cells, orb_ref, y_mate_ref, y_cross_ref, x_mate_ref, x_cross_ref):
    lines = orb_ref.shape[0] // y_cells
    odd = lax.axis_index("dy") % 2
    high = y_cells - reach
    for i in range(reach):
        y_mate_ref[i] = orb_ref[pl.ds((1 - odd) * high + i, lines, stride=y_cells), :]
        y_cross_ref[i] = orb_ref[pl.ds(odd * high + i, lines, stride=y_cells), :]
    odd = lax.axis_index("dx") % 2
    high = (x_cells - reach) * y_cells
    for b in range(lines // x_cells):
        base = b * x_cells * y_cells
        x_mate_ref[b] = orb_ref[pl.ds(pl.multiple_of(base + (1 - odd) * high, 8), reach * y_cells), :]
        x_cross_ref[b] = orb_ref[pl.ds(pl.multiple_of(base + odd * high, 8), reach * y_cells), :]


def stencil_kernel(x_cells, y_cells, orb_ref, ymat_ref, zmat_ref, acc_ref):
    rows, z_cells = orb_ref.shape
    tile = ymat_ref.shape[1]
    for start in range(0, rows, tile):
        block = orb_ref[pl.ds(start, tile), :]
        coarse = block.astype(jnp.bfloat16)
        fine = (block - coarse.astype(jnp.float32)).astype(jnp.bfloat16)
        both = jnp.concatenate([coarse, fine], axis=1)
        along_z = jnp.dot(both, zmat_ref[...], preferred_element_type=jnp.float32)
        along_y = jnp.dot(ymat_ref[...], both, preferred_element_type=jnp.float32)
        acc_ref[pl.ds(start, tile), :] = (
            (along_z[:, :z_cells] + along_y[:tile, :z_cells])
            + (along_z[:, z_cells:] + along_y[:tile, z_cells:])
            + along_y[tile:, :z_cells]
        )
    for b in range(rows // (x_cells * y_cells)):
        for y in range(0, y_cells, 8):
            column = [orb_ref[pl.ds((b * x_cells + x) * y_cells + y, 8), :] for x in range(x_cells)]
            for x in range(x_cells):
                here = pl.ds((b * x_cells + x) * y_cells + y, 8)
                total = acc_ref[here, :]
                for offset in range(1, reach + 1):
                    pair = [column[t] for t in (x - offset, x + offset) if 0 <= t < x_cells]
                    total = total + scaled[offset] * sum(pair[1:], pair[0])
                acc_ref[here, :] = total


def base_kernel(keep_ref, extra_ref, core_ref, ext_ref, dens_ref, extp_ref, parcel_ref):
    half, shared = keep_ref.shape[0], extra_ref.shape[0]
    own = lax.axis_index("band")
    for x in range(half):
        first, second = x + half * own, x + half * (1 - own)
        density = keep_ref[x] + jnp.concatenate([core_ref[first], core_ref[second]], axis=1)
        external = jnp.concatenate([ext_ref[first], ext_ref[second]], axis=1)
        dens_ref[x] = density
        extp_ref[x] = external
        t = x - (half - shared)
        if t >= 0:
            parcel_ref[t] = extra_ref[t]
            parcel_ref[shared + t] = density
            parcel_ref[2 * shared + t] = external


def exchange_lda(external, density):
    return external - slater * jnp.exp(jnp.log(density) * (1.0 / 3.0))


def potential_kernel(dens_ref, extp_ref, came_ref, pot_ref):
    for x in range(pot_ref.shape[0]):
        pot_ref[x] = exchange_lda(extp_ref[x], dens_ref[x] + came_ref[x])


def owned_kernel(dens_ref, extp_ref, extra_ref, parcel_ref, pot_ref, mine_ref, theirs_ref, out_ref):
    half, _, z_cells = dens_ref.shape
    late, shared = pot_ref.shape[0], mine_ref.shape[0]
    own = lax.axis_index("band")
    for t in range(shared):
        mine_ref[t] = exchange_lda(extp_ref[late + t], dens_ref[late + t] + parcel_ref[t])
        theirs_ref[t] = exchange_lda(parcel_ref[2 * shared + t], parcel_ref[shared + t] + extra_ref[t])
    for x in range(half):
        first, second = x + half * own, x + half * (1 - own)
        value = pot_ref[x] if x < late else mine_ref[x - late]
        out_ref[first] = value[:, : z_cells // 2]
        out_ref[second] = value[:, z_cells // 2 :]


def x_border_kernel(x_cells, y_cells, mate, inner_ref, face_ref, acc_ref):
    odd = lax.axis_index("dx") % 2
    upper = 1 - odd if mate else odd
    for b in range(inner_ref.shape[0] // (x_cells * y_cells)):
        for k in range(reach):
            x = b * x_cells + k + upper * (x_cells - 1 - 2 * k)
            here = pl.ds(pl.multiple_of(x * y_cells, 8), y_cells)
            total = inner_ref[here, :]
            for offset in range(k + 1, reach + 1):
                m = offset - 1 - k
                row = (reach - 1 - m + upper * (2 * m + 1 - reach)) * y_cells
                total = total + scaled[offset] * face_ref[b, pl.ds(pl.multiple_of(row, 8), y_cells), :]
            acc_ref[here, :] = total


def y_border_kernel(x_cells, y_cells, mate_ref, cross_ref, matrix_ref, inner_ref, acc_ref):
    odd = lax.axis_index("dy") % 2
    for face_ref, upper in ((mate_ref, 1 - odd), (cross_ref, odd)):
        matrix = matrix_ref[upper]
        for first in range(0, face_ref.shape[1], 8):
            block = jnp.concatenate([face_ref[i, pl.ds(first, 8), :] for i in range(reach)], axis=0)
            coarse = block.astype(jnp.bfloat16)
            fine = (block - coarse.astype(jnp.float32)).astype(jnp.bfloat16)
            added = jnp.dot(
                matrix, jnp.concatenate([coarse, fine, coarse], axis=0), preferred_element_type=jnp.float32
            )
            for line in range(8):
                row = (first + line) * y_cells + upper * (y_cells - 8)
                here = pl.ds(pl.multiple_of(row, 8), 8)
                acc_ref[here, :] = inner_ref[here, :] + added[8 * line : 8 * line + 8]


def final_kernel(
    x_cells, y_cells, orb_ref, acc_ref, mine_ref, theirs_ref, late_mine_ref, came_ref, out_ref, held_ref, sems
):
    z_cells = orb_ref.shape[1]
    bands = orb_ref.shape[0] // (x_cells * y_cells)
    own = own_lanes((y_cells, z_cells))
    half, part, late = x_cells // 2, x_cells // 8, came_ref.shape[0]
    copies = []
    for x in range(half):
        if x < late:
            mine, came = late_mine_ref[x], came_ref[x]
        else:
            mine, came = mine_ref[x - late], theirs_ref[x - late]
        near = jnp.where(own, mine, came)
        far = pltpu.roll(jnp.where(own, came, mine), z_cells // 2, 1)
        for t, potential in ((x, near), (x + half, far)):
            for b in range(bands):
                here = pl.ds((b * x_cells + t) * y_cells, y_cells)
                held_ref[here, :] = acc_ref[here, :] + potential * orb_ref[here, :]
        if x % part == part - 1:
            for first in (x + 1 - part, x + 1 - part + half):
                for b in range(bands):
                    piece = pl.ds((b * x_cells + first) * y_cells, part * y_cells)
                    copy = pltpu.make_async_copy(
                        held_ref.at[piece, :], out_ref.at[piece, :], sems.at[len(copies)]
                    )
                    copy.start()
                    copies.append(copy)
    for copy in copies:
        copy.wait()


def whole_kernel(orb_ref, acc_ref, potential_ref, out_ref):
    planes, y_cells, _ = potential_ref.shape
    for line in range(orb_ref.shape[0] // y_cells):
        here = pl.ds(line * y_cells, y_cells)
        out_ref[here, :] = acc_ref[here, :] + potential_ref[line % planes] * orb_ref[here, :]


def band_matrix(size, extent, periodic):
    matrix = np.zeros((size, size), np.float32)
    for i in range(size):
        group = i // extent * extent
        for offset in range(-reach, reach + 1):
            j = i - group + offset
            if periodic:
                j %= extent
            if 0 <= j < extent:
                matrix[i, group + j] += scaled[abs(offset)]
    return matrix


def face_matrix(upper):
    matrix = np.zeros((8, 8, reach, 8), np.float32)
    for k in range(reach):
        for offset in range(k + 1, reach + 1):
            m = offset - 1 - k
            line, source = (7 - k, m) if upper else (k, reach - 1 - m)
            for plane in range(8):
                matrix[plane, line, source, plane] = scaled[offset]
    return matrix.reshape(64, 8 * reach)


def split_constant(matrix):
    coarse = matrix.astype(jnp.bfloat16)
    return coarse, (matrix - coarse.astype(np.float32)).astype(jnp.bfloat16)


def call(kernel, outs, args, spaces=None, out_spaces=None, scratch=(), flops=1 << 20, aliases=None):
    shapes = [jax.ShapeDtypeStruct(shape, jnp.float32) for shape in outs]
    spaces = spaces or [pltpu.VMEM] * len(args)
    out_spaces = out_spaces or [pltpu.VMEM] * len(outs)
    return pl.pallas_call(
        kernel,
        out_shape=shapes,
        in_specs=[pl.BlockSpec(memory_space=space) for space in spaces],
        out_specs=[pl.BlockSpec(memory_space=space) for space in out_spaces],
        scratch_shapes=list(scratch),
        input_output_aliases=aliases or {},
        cost_estimate=pl.CostEstimate(flops=flops, bytes_accessed=0, transcendentals=0),
        compiler_params=pltpu.CompilerParams(vmem_limit_bytes=16 << 20),
    )(*args)


def on_device(orbitals, occupations, core_density, external):
    bands, x_cells, y_cells, z_cells = orbitals.shape
    rows = bands * x_cells * y_cells
    orb = pltpu.with_memory_space_constraint(orbitals.reshape(rows, z_cells), pltpu.HBM)
    flat = (rows, z_cells)
    y_halo = (reach, bands * x_cells, z_cells)
    x_halo = (bands, reach * y_cells, z_cells)
    bind = lambda kernel: functools.partial(kernel, x_cells, y_cells)
    paired = lax.axis_size("band") == 2
    if paired:
        half = x_cells // 2
        shared = half * 3 // 16
        late = half - shared
        planes = lambda count: (count, y_cells, z_cells)
        orb, keep, send, extra = call(
            bind(density_kernel),
            [flat, planes(half), planes(late), planes(shared)],
            [pltpu.with_memory_space_constraint(occupations, pltpu.HBM), orb],
            spaces=[pltpu.HBM, pltpu.HBM],
            scratch=[
                pltpu.SMEM(occupations.shape, jnp.float32),
                pltpu.SemaphoreType.DMA,
                pltpu.SemaphoreType.DMA((8 * bands,)),
            ],
        )
        came = exchanged(send, "band", 0)
    y_mate, y_cross, mate, cross = call(
        bind(halo_kernel), [y_halo, y_halo, x_halo, x_halo], [orb]
    )
    y_mate, y_cross = exchanged(y_mate, "dy", 0), exchanged(y_cross, "dy", 1)
    cross = exchanged(cross, "dx", 1)
    if paired:
        dens, extp, parcel = call(
            base_kernel,
            [planes(half), planes(half), planes(3 * shared)],
            [keep, extra, core_density, external],
        )
        parcel = exchanged(parcel, "band", 0)
        (late_mine,) = call(potential_kernel, [planes(late)], [dens, extp, came])
        came = exchanged(late_mine, "band", 0)
        orb, late_mine = lax.optimization_barrier((orb, late_mine))
    else:
        own_density = jnp.sum(occupations[:, None, None, None] * orbitals * orbitals, axis=0)
        total = lax.psum_scatter(own_density, "band", scatter_dimension=2, tiled=True)
        owned = external - slater * (total + core_density) ** (1.0 / 3.0)
        potential = lax.all_gather(owned, "band", axis=2, tiled=True)
    tile = 8 * y_cells
    middle = np.float32(scaled[0]) * np.eye(tile, dtype=np.float32)
    coarse, fine = split_constant(band_matrix(tile, y_cells, False) + middle)
    ymat = np.concatenate([coarse, fine], axis=0)
    coarse, fine = split_constant(band_matrix(z_cells, z_cells, True))
    zmat = np.block([[coarse, fine], [coarse, np.zeros_like(fine)]])
    (acc,) = call(
        bind(stencil_kernel), [flat], [orb, jnp.asarray(ymat), jnp.asarray(zmat)], flops=1 << 28
    )
    acc, mate = lax.optimization_barrier((acc, mate))
    mate = exchanged(mate, "dx", 0)
    if paired:
        acc, dens = lax.optimization_barrier((acc, dens))
        mine, theirs, owned = call(
            owned_kernel,
            [planes(shared), planes(shared), core_density.shape],
            [dens, extp, extra, parcel, late_mine],
        )
        acc, owned = lax.optimization_barrier((acc, owned))
    border = lambda which: functools.partial(x_border_kernel, x_cells, y_cells, which)
    sides = []
    for upper in (False, True):
        coarse, fine = split_constant(face_matrix(upper))
        sides.append(np.concatenate([coarse, coarse, fine], axis=1))
    (acc,) = call(
        bind(y_border_kernel), [flat], [y_mate, y_cross, jnp.asarray(np.stack(sides)), acc], aliases={3: 0}, flops=FY
    )
    (acc,) = call(border(False), [flat], [acc, cross], aliases={0: 0}, flops=FX)
    (acc,) = call(border(True), [flat], [acc, mate], aliases={0: 0}, flops=FM)
    if paired:
        (applied,) = call(
            bind(final_kernel),
            [flat],
            [orb, acc, mine, theirs, late_mine, came],
            out_spaces=[pltpu.HBM],
            scratch=[pltpu.VMEM(flat, jnp.float32), pltpu.SemaphoreType.DMA((8 * bands,))],
        )
    else:
        (applied,) = call(whole_kernel, [flat], [orb, acc, potential])
    return applied.reshape(orbitals.shape), owned


def solution(mesh):
    return jax.shard_map(
        on_device,
        mesh=mesh,
        in_specs=(
            P("band", "dx", "dy", None),
            P("band"),
            P("dx", "dy", "band"),
            P("dx", "dy", "band"),
        ),
        out_specs=(P("band", "dx", "dy", None), P("dx", "dy", "band")),
        check_vma=False,
    )
```

```python
import functools
import math

import jax
import jax.numpy as jnp
import numpy as np
from jax import lax
from jax.experimental import pallas as pl
from jax.experimental.pallas import tpu as pltpu
from jax.sharding import PartitionSpec as P

coeffs = (
    -5369.0 / 1800.0,
    12.0 / 7.0,
    -15.0 / 56.0,
    10.0 / 189.0,
    -1.0 / 112.0,
    2.0 / 1925.0,
    -1.0 / 16632.0,
)
reach = len(coeffs) - 1
grid_step = 2.0
slater = (3.0 / math.pi) ** (1.0 / 3.0)
scaled = tuple(-0.5 * c / (grid_step * grid_step) for c in coeffs)


def shifted(block, axis, up):
    count = lax.axis_size(axis)
    pairs = [(i, (i + 1) % count) for i in range(count)]
    if not up:
        pairs = [(target, source) for source, target in pairs]
    return lax.ppermute(block, axis, pairs)


def own_lanes(shape):
    lane = lax.broadcasted_iota(jnp.int32, shape, 1)
    return (lane < shape[1] // 2) == (lax.axis_index("band") == 0)


def fetch_copies(x_cells, y_cells, source_ref, target_ref, sems):
    bands = source_ref.shape[0] // (x_cells * y_cells)
    quarter = x_cells // 4 * y_cells
    return [
        [
            pltpu.make_async_copy(
                source_ref.at[pl.ds((4 * b + q) * quarter, quarter), :],
                target_ref.at[pl.ds((4 * b + q) * quarter, quarter), :],
                sems.at[4 * b + q],
            )
            for b in range(bands)
            for q in (part, part + 2)
        ]
        for part in range(2)
    ]


def density_kernel(
    x_cells, y_cells, occ_ref, source_ref, orb_ref, keep_ref, send_ref, *rest
):
    *halo_refs, weight_ref, weight_sem, sems = rest
    weights = pltpu.make_async_copy(occ_ref, weight_ref, weight_sem)
    weights.start()
    copies = fetch_copies(x_cells, y_cells, source_ref, orb_ref, sems)
    for part in copies:
        for copy in part:
            copy.start()
    z_cells = orb_ref.shape[1]
    bands = orb_ref.shape[0] // (x_cells * y_cells)
    own = own_lanes((y_cells, z_cells))

    def summed(x):
        total = None
        for b in range(bands):
            value = orb_ref[pl.ds((b * x_cells + x) * y_cells, y_cells), :]
            term = weight_ref[b] * value * value
            total = term if total is None else total + term
        return total

    weights.wait()
    for part in range(2):
        for copy in copies[part]:
            copy.wait()
        for x in range(part * x_cells // 4, (part + 1) * x_cells // 4):
            near = summed(x)
            far = pltpu.roll(summed(x + x_cells // 2), z_cells // 2, 1)
            keep_ref[x] = jnp.where(own, near, far)
            send_ref[x] = jnp.where(own, far, near)
    halo_kernel(x_cells, y_cells, orb_ref, *halo_refs)


def halo_kernel(x_cells, y_cells, orb_ref, ylow_ref, yhigh_ref, xlow_ref, xhigh_ref):
    lines = orb_ref.shape[0] // y_cells
    for i in range(reach):
        ylow_ref[i] = orb_ref[pl.ds(y_cells - reach + i, lines, stride=y_cells), :]
        yhigh_ref[i] = orb_ref[pl.ds(i, lines, stride=y_cells), :]
    span, brick = reach * y_cells, x_cells * y_cells
    for b in range(lines // x_cells):
        xlow_ref[b] = orb_ref[pl.ds((b + 1) * brick - span, span), :]
        xhigh_ref[b] = orb_ref[pl.ds(b * brick, span), :]


def stencil_kernel(x_cells, y_cells, orb_ref, ymat_ref, zmat_ref, acc_ref):
    rows, z_cells = orb_ref.shape
    tile = ymat_ref.shape[1]
    for start in range(0, rows, tile):
        block = orb_ref[pl.ds(start, tile), :]
        coarse = block.astype(jnp.bfloat16)
        fine = (block - coarse.astype(jnp.float32)).astype(jnp.bfloat16)
        both = jnp.concatenate([coarse, fine], axis=1)
        along_z = jnp.dot(both, zmat_ref[...], preferred_element_type=jnp.float32)
        along_y = jnp.dot(ymat_ref[...], both, preferred_element_type=jnp.float32)
        acc_ref[pl.ds(start, tile), :] = (
            (along_z[:, :z_cells] + along_y[:tile, :z_cells])
            + (along_z[:, z_cells:] + along_y[:tile, z_cells:])
            + along_y[tile:, :z_cells]
        )
    for b in range(rows // (x_cells * y_cells)):
        for y in range(0, y_cells, 8):
            column = [orb_ref[pl.ds((b * x_cells + x) * y_cells + y, 8), :] for x in range(x_cells)]
            for x in range(x_cells):
                here = pl.ds((b * x_cells + x) * y_cells + y, 8)
                total = acc_ref[here, :]
                for offset in range(1, reach + 1):
                    pair = [column[t] for t in (x - offset, x + offset) if 0 <= t < x_cells]
                    total = total + scaled[offset] * sum(pair[1:], pair[0])
                acc_ref[here, :] = total


def base_kernel(keep_ref, core_ref, ext_ref, dens_ref, extp_ref):
    half = keep_ref.shape[0]
    own = lax.axis_index("band")
    for x in range(half):
        first, second = x + half * own, x + half * (1 - own)
        dens_ref[x] = keep_ref[x] + jnp.concatenate([core_ref[first], core_ref[second]], axis=1)
        extp_ref[x] = jnp.concatenate([ext_ref[first], ext_ref[second]], axis=1)


def potential_kernel(dens_ref, extp_ref, came_ref, pot_ref):
    for x in range(dens_ref.shape[0]):
        density = dens_ref[x] + came_ref[x]
        pot_ref[x] = extp_ref[x] - slater * jnp.exp(jnp.log(density) * (1.0 / 3.0))


def owned_kernel(pot_ref, out_ref):
    half, _, z_cells = pot_ref.shape
    own = lax.axis_index("band")
    for x in range(half):
        first, second = x + half * own, x + half * (1 - own)
        value = pot_ref[x]
        out_ref[first] = value[:, : z_cells // 2]
        out_ref[second] = value[:, z_cells // 2 :]


def border_kernel(x_cells, y_cells, inner_ref, yhigh_ref, ylow_ref, xlow_ref, xhigh_ref, acc_ref):
    lines = inner_ref.shape[0] // y_cells
    for line in range(lines):
        b, x = divmod(line, x_cells)
        if reach <= x < x_cells - reach:
            continue
        here = pl.ds(line * y_cells, y_cells)
        total = inner_ref[here, :]
        for offset in range(1, reach + 1):
            if x - offset < 0:
                row = (reach + x - offset) * y_cells
                total = total + scaled[offset] * xlow_ref[b, pl.ds(row, y_cells), :]
            if x + offset >= x_cells:
                row = (x + offset - x_cells) * y_cells
                total = total + scaled[offset] * xhigh_ref[b, pl.ds(row, y_cells), :]
        acc_ref[here, :] = total
    for y in range(reach):
        low = pl.ds(y, lines, stride=y_cells)
        high = pl.ds(y_cells - 1 - y, lines, stride=y_cells)
        low_sum, high_sum = acc_ref[low, :], acc_ref[high, :]
        for offset in range(y + 1, reach + 1):
            low_sum = low_sum + scaled[offset] * ylow_ref[reach + y - offset]
            high_sum = high_sum + scaled[offset] * yhigh_ref[offset - 1 - y]
        acc_ref[low, :] = low_sum
        acc_ref[high, :] = high_sum


def final_kernel(x_cells, y_cells, orb_ref, acc_ref, mine_ref, came_ref, out_ref, held_ref, sems):
    z_cells = orb_ref.shape[1]
    bands = orb_ref.shape[0] // (x_cells * y_cells)
    own = own_lanes((y_cells, z_cells))
    half, part = x_cells // 2, x_cells // 8
    copies = []
    for x in range(half):
        mine, came = mine_ref[x], came_ref[x]
        near = jnp.where(own, mine, came)
        far = pltpu.roll(jnp.where(own, came, mine), z_cells // 2, 1)
        for t, potential in ((x, near), (x + half, far)):
            for b in range(bands):
                here = pl.ds((b * x_cells + t) * y_cells, y_cells)
                held_ref[here, :] = acc_ref[here, :] + potential * orb_ref[here, :]
        if x % part == part - 1:
            for first in (x + 1 - part, x + 1 - part + half):
                for b in range(bands):
                    piece = pl.ds((b * x_cells + first) * y_cells, part * y_cells)
                    copy = pltpu.make_async_copy(
                        held_ref.at[piece, :], out_ref.at[piece, :], sems.at[len(copies)]
                    )
                    copy.start()
                    copies.append(copy)
    for copy in copies:
        copy.wait()


def whole_kernel(orb_ref, acc_ref, potential_ref, out_ref):
    planes, y_cells, _ = potential_ref.shape
    for line in range(orb_ref.shape[0] // y_cells):
        here = pl.ds(line * y_cells, y_cells)
        out_ref[here, :] = acc_ref[here, :] + potential_ref[line % planes] * orb_ref[here, :]


def band_matrix(size, extent, periodic):
    matrix = np.zeros((size, size), np.float32)
    for i in range(size):
        group = i // extent * extent
        for offset in range(-reach, reach + 1):
            j = i - group + offset
            if periodic:
                j %= extent
            if 0 <= j < extent:
                matrix[i, group + j] += scaled[abs(offset)]
    return matrix


def split_constant(matrix):
    coarse = matrix.astype(jnp.bfloat16)
    return coarse, (matrix - coarse.astype(np.float32)).astype(jnp.bfloat16)


def call(kernel, outs, args, spaces=None, out_spaces=None, scratch=(), flops=1 << 20, aliases=None):
    shapes = [jax.ShapeDtypeStruct(shape, jnp.float32) for shape in outs]
    moved = sum(4 * math.prod(shape) for shape in outs) + sum(4 * a.size for a in args)
    spaces = spaces or [pltpu.VMEM] * len(args)
    out_spaces = out_spaces or [pltpu.VMEM] * len(outs)
    return pl.pallas_call(
        kernel,
        out_shape=shapes,
        in_specs=[pl.BlockSpec(memory_space=space) for space in spaces],
        out_specs=[pl.BlockSpec(memory_space=space) for space in out_spaces],
        scratch_shapes=list(scratch),
        input_output_aliases=aliases or {},
        cost_estimate=pl.CostEstimate(flops=flops, bytes_accessed=moved, transcendentals=0),
        compiler_params=pltpu.CompilerParams(vmem_limit_bytes=16 << 20),
    )(*args)


def on_device(orbitals, occupations, core_density, external):
    bands, x_cells, y_cells, z_cells = orbitals.shape
    rows = bands * x_cells * y_cells
    orb = pltpu.with_memory_space_constraint(orbitals.reshape(rows, z_cells), pltpu.HBM)
    flat = (rows, z_cells)
    y_halo = (reach, bands * x_cells, z_cells)
    x_halo = (bands, reach * y_cells, z_cells)
    bind = lambda kernel: functools.partial(kernel, x_cells, y_cells)
    paired = lax.axis_size("band") == 2
    if paired:
        packed = (x_cells // 2, y_cells, z_cells)
        orb, keep, send, *halos = call(
            bind(density_kernel),
            [flat, packed, packed, y_halo, y_halo, x_halo, x_halo],
            [pltpu.with_memory_space_constraint(occupations, pltpu.HBM), orb],
            spaces=[pltpu.HBM, pltpu.HBM],
            scratch=[
                pltpu.SMEM(occupations.shape, jnp.float32),
                pltpu.SemaphoreType.DMA,
                pltpu.SemaphoreType.DMA((4 * bands,)),
            ],
        )
        came = shifted(send, "band", True)
    else:
        halos = call(bind(halo_kernel), [y_halo, y_halo, x_halo, x_halo], [orb])
    ylow, yhigh, xlow, xhigh = halos
    xlow, xhigh = shifted(xlow, "dx", True), shifted(xhigh, "dx", False)
    ylow, yhigh = shifted(ylow, "dy", True), shifted(yhigh, "dy", False)
    if paired:
        dens, extp = call(base_kernel, [packed, packed], [keep, core_density, external])
        (mine,) = call(potential_kernel, [packed], [dens, extp, came])
        came = shifted(mine, "band", True)
        (owned,) = call(owned_kernel, [core_density.shape], [mine])
        orb, mine = lax.optimization_barrier((orb, mine))
    else:
        own_density = jnp.sum(occupations[:, None, None, None] * orbitals * orbitals, axis=0)
        shared = lax.psum_scatter(own_density, "band", scatter_dimension=2, tiled=True)
        owned = external - slater * (shared + core_density) ** (1.0 / 3.0)
        potential = lax.all_gather(owned, "band", axis=2, tiled=True)
    tile = 8 * y_cells
    middle = np.float32(scaled[0]) * np.eye(tile, dtype=np.float32)
    coarse, fine = split_constant(band_matrix(tile, y_cells, False) + middle)
    ymat = np.concatenate([coarse, fine], axis=0)
    coarse, fine = split_constant(band_matrix(z_cells, z_cells, True))
    zmat = np.block([[coarse, fine], [coarse, np.zeros_like(fine)]])
    (acc,) = call(
        bind(stencil_kernel), [flat], [orb, jnp.asarray(ymat), jnp.asarray(zmat)], flops=1 << 28
    )
    if paired:
        acc, owned = lax.optimization_barrier((acc, owned))
    (acc,) = call(bind(border_kernel), [flat], [acc, yhigh, ylow, xlow, xhigh], aliases={0: 0}, flops=1 << 34)
    if paired:
        (applied,) = call(
            bind(final_kernel),
            [flat],
            [orb, acc, mine, came],
            out_spaces=[pltpu.HBM],
            scratch=[pltpu.VMEM(flat, jnp.float32), pltpu.SemaphoreType.DMA((8 * bands,))],
        )
    else:
        (applied,) = call(whole_kernel, [flat], [orb, acc, potential])
    return applied.reshape(orbitals.shape), owned


def solution(mesh):
    return jax.shard_map(
        on_device,
        mesh=mesh,
        in_specs=(
            P("band", "dx", "dy", None),
            P("band"),
            P("dx", "dy", "band"),
            P("dx", "dy", "band"),
        ),
        out_specs=(P("band", "dx", "dy", None), P("dx", "dy", "band")),
        check_vma=False,
    )
```

```python
import functools
import math

import jax
import jax.numpy as jnp
import numpy as np
from jax import lax
from jax.experimental import pallas as pl
from jax.experimental.pallas import tpu as pltpu
from jax.sharding import PartitionSpec as P

coeffs = (
    -5369.0 / 1800.0,
    12.0 / 7.0,
    -15.0 / 56.0,
    10.0 / 189.0,
    -1.0 / 112.0,
    2.0 / 1925.0,
    -1.0 / 16632.0,
)
reach = len(coeffs) - 1
grid_step = 2.0
slater = (3.0 / math.pi) ** (1.0 / 3.0)
scaled = tuple(-0.5 * c / (grid_step * grid_step) for c in coeffs)


def exchanged(block, axis, first):
    count = lax.axis_size(axis)
    pairs = [((first + i) % count, (first + (i ^ 1)) % count) for i in range(count)]
    return lax.ppermute(block, axis, pairs)


def shifted(block, axis, up):
    count = lax.axis_size(axis)
    pairs = [(i, (i + 1) % count) if up else ((i + 1) % count, i) for i in range(count)]
    return lax.ppermute(block, axis, pairs)


def own_lanes(shape):
    lane = lax.broadcasted_iota(jnp.int32, shape, 1)
    return (lane < shape[1] // 2) == (lax.axis_index("band") == 0)


def density_kernel(x_cells, y_cells, occ_ref, source_ref, orb_ref, keep_ref, send_ref, weight_ref, weight_sem, sems):
    rows, z_cells = orb_ref.shape
    bands, half = rows // (x_cells * y_cells), x_cells // 2
    group = half // 4
    weights = pltpu.make_async_copy(occ_ref, weight_ref, weight_sem)
    weights.start()
    copies = []
    for part in range(4):
        for b in range(bands):
            for first in (part * group, part * group + half):
                piece = pl.ds((b * x_cells + first) * y_cells, group * y_cells)
                copies.append(
                    pltpu.make_async_copy(source_ref.at[piece, :], orb_ref.at[piece, :], sems.at[len(copies)])
                )
                copies[-1].start()
    own = own_lanes((y_cells, z_cells))

    def summed(x):
        total = None
        for b in range(bands):
            value = orb_ref[pl.ds((b * x_cells + x) * y_cells, y_cells), :]
            term = weight_ref[b] * value * value
            total = term if total is None else total + term
        return total

    weights.wait()
    for part in range(4):
        for copy in copies[2 * bands * part : 2 * bands * (part + 1)]:
            copy.wait()
        for x in range(part * group, (part + 1) * group):
            near = summed(x)
            far = pltpu.roll(summed(x + half), z_cells // 2, 1)
            keep_ref[x] = jnp.where(own, near, far)
            send_ref[x] = jnp.where(own, far, near)


def halo_kernel(x_cells, y_cells, orb_ref, y_mate_ref, y_cross_ref, x_mate_ref, x_cross_ref):
    lines = orb_ref.shape[0] // y_cells
    odd = lax.axis_index("dy") % 2
    high = y_cells - reach
    for i in range(reach):
        y_mate_ref[i] = orb_ref[pl.ds(high + i, lines, stride=y_cells), :]
        y_cross_ref[i] = orb_ref[pl.ds(i, lines, stride=y_cells), :]
    odd = lax.axis_index("dx") % 2
    high = (x_cells - reach) * y_cells
    for b in range(lines // x_cells):
        base = b * x_cells * y_cells
        x_mate_ref[b] = orb_ref[pl.ds(base + high, reach * y_cells), :]
        x_cross_ref[b] = orb_ref[pl.ds(base, reach * y_cells), :]


def stencil_kernel(x_cells, y_cells, orb_ref, ymat_ref, zmat_ref, acc_ref):
    rows, z_cells = orb_ref.shape
    tile = ymat_ref.shape[1]
    for start in range(0, rows, tile):
        block = orb_ref[pl.ds(start, tile), :]
        coarse = block.astype(jnp.bfloat16)
        fine = (block - coarse.astype(jnp.float32)).astype(jnp.bfloat16)
        both = jnp.concatenate([coarse, fine], axis=1)
        along_z = jnp.dot(both, zmat_ref[...], preferred_element_type=jnp.float32)
        along_y = jnp.dot(ymat_ref[...], both, preferred_element_type=jnp.float32)
        acc_ref[pl.ds(start, tile), :] = (
            (along_z[:, :z_cells] + along_y[:tile, :z_cells])
            + (along_z[:, z_cells:] + along_y[:tile, z_cells:])
            + along_y[tile:, :z_cells]
        )
    for b in range(rows // (x_cells * y_cells)):
        for y in range(0, y_cells, 8):
            column = [orb_ref[pl.ds((b * x_cells + x) * y_cells + y, 8), :] for x in range(x_cells)]
            for x in range(x_cells):
                here = pl.ds((b * x_cells + x) * y_cells + y, 8)
                total = acc_ref[here, :]
                for offset in range(1, reach + 1):
                    pair = [column[t] for t in (x - offset, x + offset) if 0 <= t < x_cells]
                    total = total + scaled[offset] * sum(pair[1:], pair[0])
                acc_ref[here, :] = total


def base_kernel(keep_ref, core_ref, ext_ref, dens_ref, extp_ref):
    half = keep_ref.shape[0]
    own = lax.axis_index("band")
    for x in range(half):
        first, second = x + half * own, x + half * (1 - own)
        dens_ref[x] = keep_ref[x] + jnp.concatenate([core_ref[first], core_ref[second]], axis=1)
        extp_ref[x] = jnp.concatenate([ext_ref[first], ext_ref[second]], axis=1)


def potential_kernel(dens_ref, extp_ref, came_ref, pot_ref):
    for x in range(pot_ref.shape[0]):
        density = dens_ref[x] + came_ref[x]
        pot_ref[x] = extp_ref[x] - slater * jnp.exp(jnp.log(density) * (1.0 / 3.0))


def owned_kernel(pot_ref, out_ref):
    half, _, z_cells = pot_ref.shape
    own = lax.axis_index("band")
    for x in range(half):
        first, second = x + half * own, x + half * (1 - own)
        value = pot_ref[x]
        out_ref[first] = value[:, : z_cells // 2]
        out_ref[second] = value[:, z_cells // 2 :]


def x_border_kernel(x_cells, y_cells, mate, inner_ref, face_ref, acc_ref):
    odd = lax.axis_index("dx") % 2
    upper = 0 if mate else 1
    for b in range(inner_ref.shape[0] // (x_cells * y_cells)):
        for k in range(reach):
            x = b * x_cells + k + upper * (x_cells - 1 - 2 * k)
            here = pl.ds(pl.multiple_of(x * y_cells, 8), y_cells)
            total = inner_ref[here, :]
            for offset in range(k + 1, reach + 1):
                m = offset - 1 - k
                row = (reach - 1 - m + upper * (2 * m + 1 - reach)) * y_cells
                total = total + scaled[offset] * face_ref[b, pl.ds(pl.multiple_of(row, 8), y_cells), :]
            acc_ref[here, :] = total


def y_border_kernel(x_cells, y_cells, cross_ref, mate_ref, matrix_ref, inner_ref, acc_ref):
    odd = lax.axis_index("dy") % 2
    for face_ref, upper in ((mate_ref, 0), (cross_ref, 1)):
        matrix = matrix_ref[upper]
        for first in range(0, face_ref.shape[1], 8):
            block = jnp.concatenate([face_ref[i, pl.ds(first, 8), :] for i in range(reach)], axis=0)
            coarse = block.astype(jnp.bfloat16)
            fine = (block - coarse.astype(jnp.float32)).astype(jnp.bfloat16)
            added = jnp.dot(
                matrix, jnp.concatenate([coarse, fine, coarse], axis=0), preferred_element_type=jnp.float32
            )
            for line in range(8):
                row = (first + line) * y_cells + upper * (y_cells - 8)
                here = pl.ds(pl.multiple_of(row, 8), 8)
                acc_ref[here, :] = inner_ref[here, :] + added[8 * line : 8 * line + 8]


def final_kernel(
    x_cells, y_cells, orb_ref, acc_ref, mine_ref, came_ref, out_ref, held_ref, sems
):
    z_cells = orb_ref.shape[1]
    bands = orb_ref.shape[0] // (x_cells * y_cells)
    own = own_lanes((y_cells, z_cells))
    half, part = x_cells // 2, x_cells // 8
    copies = []
    for x in range(half):
        mine, came = mine_ref[x], came_ref[x]
        near = jnp.where(own, mine, came)
        far = pltpu.roll(jnp.where(own, came, mine), z_cells // 2, 1)
        for t, potential in ((x, near), (x + half, far)):
            for b in range(bands):
                here = pl.ds((b * x_cells + t) * y_cells, y_cells)
                held_ref[here, :] = acc_ref[here, :] + potential * orb_ref[here, :]
        if x % part == part - 1:
            for first in (x + 1 - part, x + 1 - part + half):
                for b in range(bands):
                    piece = pl.ds((b * x_cells + first) * y_cells, part * y_cells)
                    copy = pltpu.make_async_copy(
                        held_ref.at[piece, :], out_ref.at[piece, :], sems.at[len(copies)]
                    )
                    copy.start()
                    copies.append(copy)
    for copy in copies:
        copy.wait()


def whole_kernel(orb_ref, acc_ref, potential_ref, out_ref):
    planes, y_cells, _ = potential_ref.shape
    for line in range(orb_ref.shape[0] // y_cells):
        here = pl.ds(line * y_cells, y_cells)
        out_ref[here, :] = acc_ref[here, :] + potential_ref[line % planes] * orb_ref[here, :]


def band_matrix(size, extent, periodic):
    matrix = np.zeros((size, size), np.float32)
    for i in range(size):
        group = i // extent * extent
        for offset in range(-reach, reach + 1):
            j = i - group + offset
            if periodic:
                j %= extent
            if 0 <= j < extent:
                matrix[i, group + j] += scaled[abs(offset)]
    return matrix


def face_matrix(upper):
    matrix = np.zeros((8, 8, reach, 8), np.float32)
    for k in range(reach):
        for offset in range(k + 1, reach + 1):
            m = offset - 1 - k
            line, source = (7 - k, m) if upper else (k, reach - 1 - m)
            for plane in range(8):
                matrix[plane, line, source, plane] = scaled[offset]
    return matrix.reshape(64, 8 * reach)


def split_constant(matrix):
    coarse = matrix.astype(jnp.bfloat16)
    return coarse, (matrix - coarse.astype(np.float32)).astype(jnp.bfloat16)


def call(kernel, outs, args, spaces=None, out_spaces=None, scratch=(), flops=1 << 20, aliases=None):
    shapes = [jax.ShapeDtypeStruct(shape, jnp.float32) for shape in outs]
    spaces = spaces or [pltpu.VMEM] * len(args)
    out_spaces = out_spaces or [pltpu.VMEM] * len(outs)
    return pl.pallas_call(
        kernel,
        out_shape=shapes,
        in_specs=[pl.BlockSpec(memory_space=space) for space in spaces],
        out_specs=[pl.BlockSpec(memory_space=space) for space in out_spaces],
        scratch_shapes=list(scratch),
        input_output_aliases=aliases or {},
        cost_estimate=pl.CostEstimate(flops=flops, bytes_accessed=0, transcendentals=0),
        compiler_params=pltpu.CompilerParams(vmem_limit_bytes=16 << 20),
    )(*args)


def on_device(orbitals, occupations, core_density, external):
    bands, x_cells, y_cells, z_cells = orbitals.shape
    rows = bands * x_cells * y_cells
    orb = pltpu.with_memory_space_constraint(orbitals.reshape(rows, z_cells), pltpu.HBM)
    flat = (rows, z_cells)
    y_halo = (reach, bands * x_cells, z_cells)
    x_halo = (bands, reach * y_cells, z_cells)
    bind = lambda kernel: functools.partial(kernel, x_cells, y_cells)
    paired = lax.axis_size("band") == 2
    if paired:
        packed = (x_cells // 2, y_cells, z_cells)
        occ = pltpu.with_memory_space_constraint(occupations, pltpu.HBM)
        orb, keep, send = call(
            bind(density_kernel),
            [flat, packed, packed],
            [occ, orb],
            spaces=[pltpu.HBM, pltpu.HBM],
            scratch=[
                pltpu.SMEM(occupations.shape, jnp.float32),
                pltpu.SemaphoreType.DMA,
                pltpu.SemaphoreType.DMA((8 * bands,)),
            ],
        )
        came = exchanged(send, "band", 0)
    y_mate, y_cross, mate, cross = call(
        bind(halo_kernel), [y_halo, y_halo, x_halo, x_halo], [orb]
    )
    y_mate, y_cross = shifted(y_mate, "dy", True), shifted(y_cross, "dy", False)
    mate, cross = shifted(mate, "dx", True), shifted(cross, "dx", False)
    if paired:
        dens, extp = call(base_kernel, [packed, packed], [keep, core_density, external])
        (mine,) = call(potential_kernel, [packed], [dens, extp, came])
        came = exchanged(mine, "band", 0)
        (owned,) = call(owned_kernel, [core_density.shape], [mine])
        orb, mine, owned = lax.optimization_barrier((orb, mine, owned))
    else:
        own_density = jnp.sum(occupations[:, None, None, None] * orbitals * orbitals, axis=0)
        total = lax.psum_scatter(own_density, "band", scatter_dimension=2, tiled=True)
        owned = external - slater * (total + core_density) ** (1.0 / 3.0)
        potential = lax.all_gather(owned, "band", axis=2, tiled=True)
    tile = 8 * y_cells
    middle = np.float32(scaled[0]) * np.eye(tile, dtype=np.float32)
    coarse, fine = split_constant(band_matrix(tile, y_cells, False) + middle)
    ymat = np.concatenate([coarse, fine], axis=0)
    coarse, fine = split_constant(band_matrix(z_cells, z_cells, True))
    zmat = np.block([[coarse, fine], [coarse, np.zeros_like(fine)]])
    (acc,) = call(
        bind(stencil_kernel), [flat], [orb, jnp.asarray(ymat), jnp.asarray(zmat)], flops=1 << 28
    )
    border = lambda which: functools.partial(x_border_kernel, x_cells, y_cells, which)
    sides = []
    for upper in (False, True):
        coarse, fine = split_constant(face_matrix(upper))
        sides.append(np.concatenate([coarse, coarse, fine], axis=1))
    (acc,) = call(
        bind(y_border_kernel), [flat], [y_cross, y_mate, jnp.asarray(np.stack(sides)), acc], aliases={3: 0}, flops=0
    )
    (acc,) = call(border(False), [flat], [acc, cross], aliases={0: 0}, flops=1 << 32)
    (acc,) = call(border(True), [flat], [acc, mate], aliases={0: 0}, flops=0)
    if paired:
        (applied,) = call(
            bind(final_kernel),
            [flat],
            [orb, acc, mine, came],
            out_spaces=[pltpu.HBM],
            scratch=[pltpu.VMEM(flat, jnp.float32), pltpu.SemaphoreType.DMA((8 * bands + 1,))],
        )
    else:
        (applied,) = call(whole_kernel, [flat], [orb, acc, potential])
    return applied.reshape(orbitals.shape), owned


def solution(mesh):
    return jax.shard_map(
        on_device,
        mesh=mesh,
        in_specs=(
            P("band", "dx", "dy", None),
            P("band"),
            P("dx", "dy", "band"),
            P("dx", "dy", "band"),
        ),
        out_specs=(P("band", "dx", "dy", None), P("dx", "dy", "band")),
        check_vma=False,
    )
```

```python
import functools
import math

import jax
import jax.numpy as jnp
import numpy as np
from jax import lax
from jax.experimental import pallas as pl
from jax.experimental.pallas import tpu as pltpu
from jax.sharding import PartitionSpec as P

coeffs = (
    -5369.0 / 1800.0,
    12.0 / 7.0,
    -15.0 / 56.0,
    10.0 / 189.0,
    -1.0 / 112.0,
    2.0 / 1925.0,
    -1.0 / 16632.0,
)
reach = len(coeffs) - 1
FY, FX, FM = 1 << 20, 1 << 30, 0
grid_step = 2.0
slater = (3.0 / math.pi) ** (1.0 / 3.0)
scaled = tuple(-0.5 * c / (grid_step * grid_step) for c in coeffs)


def exchanged(block, axis, first):
    count = lax.axis_size(axis)
    pairs = [((first + i) % count, (first + (i ^ 1)) % count) for i in range(count)]
    return lax.ppermute(block, axis, pairs)


def shifted(block, axis, up):
    count = lax.axis_size(axis)
    pairs = [(i, (i + 1) % count) if up else ((i + 1) % count, i) for i in range(count)]
    return lax.ppermute(block, axis, pairs)


def own_lanes(shape):
    lane = lax.broadcasted_iota(jnp.int32, shape, 1)
    return (lane < shape[1] // 2) == (lax.axis_index("band") == 0)


def density_kernel(
    x_cells, y_cells, occ_ref, source_ref, orb_ref, keep_ref, send_ref, extra_ref, weight_ref, weight_sem, sems
):
    rows, z_cells = orb_ref.shape
    bands, half = rows // (x_cells * y_cells), x_cells // 2
    group = half // 4
    weights = pltpu.make_async_copy(occ_ref, weight_ref, weight_sem)
    weights.start()
    copies = []
    for part in range(4):
        for b in range(bands):
            for first in (part * group, part * group + half):
                piece = pl.ds((b * x_cells + first) * y_cells, group * y_cells)
                copies.append(
                    pltpu.make_async_copy(source_ref.at[piece, :], orb_ref.at[piece, :], sems.at[len(copies)])
                )
                copies[-1].start()
    own = own_lanes((y_cells, z_cells))

    def summed(x):
        total = None
        for b in range(bands):
            value = orb_ref[pl.ds((b * x_cells + x) * y_cells, y_cells), :]
            term = weight_ref[b] * value * value
            total = term if total is None else total + term
        return total

    weights.wait()
    late = send_ref.shape[0]
    for part in range(4):
        for copy in copies[2 * bands * part : 2 * bands * (part + 1)]:
            copy.wait()
        for x in range(part * group, (part + 1) * group):
            near = summed(x)
            far = pltpu.roll(summed(x + half), z_cells // 2, 1)
            keep_ref[x] = jnp.where(own, near, far)
            other = jnp.where(own, far, near)
            if x < late:
                send_ref[x] = other
            else:
                extra_ref[x - late] = other


def halo_kernel(x_cells, y_cells, orb_ref, y_mate_ref, y_cross_ref, x_mate_ref, x_cross_ref):
    lines = orb_ref.shape[0] // y_cells
    odd = lax.axis_index("dy") % 2
    high = y_cells - reach
    for i in range(reach):
        y_mate_ref[i] = orb_ref[pl.ds(high + i, lines, stride=y_cells), :]
        y_cross_ref[i] = orb_ref[pl.ds(i, lines, stride=y_cells), :]
    odd = lax.axis_index("dx") % 2
    high = (x_cells - reach) * y_cells
    for b in range(lines // x_cells):
        base = b * x_cells * y_cells
        x_mate_ref[b] = orb_ref[pl.ds(pl.multiple_of(base + (1 - odd) * high, 8), reach * y_cells), :]
        x_cross_ref[b] = orb_ref[pl.ds(pl.multiple_of(base + odd * high, 8), reach * y_cells), :]


def stencil_kernel(x_cells, y_cells, orb_ref, ymat_ref, zmat_ref, acc_ref):
    rows, z_cells = orb_ref.shape
    tile = ymat_ref.shape[1]
    for start in range(0, rows, tile):
        block = orb_ref[pl.ds(start, tile), :]
        coarse = block.astype(jnp.bfloat16)
        fine = (block - coarse.astype(jnp.float32)).astype(jnp.bfloat16)
        both = jnp.concatenate([coarse, fine], axis=1)
        along_z = jnp.dot(both, zmat_ref[...], preferred_element_type=jnp.float32)
        along_y = jnp.dot(ymat_ref[...], both, preferred_element_type=jnp.float32)
        acc_ref[pl.ds(start, tile), :] = (
            (along_z[:, :z_cells] + along_y[:tile, :z_cells])
            + (along_z[:, z_cells:] + along_y[:tile, z_cells:])
            + along_y[tile:, :z_cells]
        )
    for b in range(rows // (x_cells * y_cells)):
        for y in range(0, y_cells, 8):
            column = [orb_ref[pl.ds((b * x_cells + x) * y_cells + y, 8), :] for x in range(x_cells)]
            for x in range(x_cells):
                here = pl.ds((b * x_cells + x) * y_cells + y, 8)
                total = acc_ref[here, :]
                for offset in range(1, reach + 1):
                    pair = [column[t] for t in (x - offset, x + offset) if 0 <= t < x_cells]
                    total = total + scaled[offset] * sum(pair[1:], pair[0])
                acc_ref[here, :] = total


def base_kernel(keep_ref, extra_ref, core_ref, ext_ref, dens_ref, extp_ref, parcel_ref):
    half, shared = keep_ref.shape[0], extra_ref.shape[0]
    own = lax.axis_index("band")
    for x in range(half):
        first, second = x + half * own, x + half * (1 - own)
        density = keep_ref[x] + jnp.concatenate([core_ref[first], core_ref[second]], axis=1)
        external = jnp.concatenate([ext_ref[first], ext_ref[second]], axis=1)
        dens_ref[x] = density
        extp_ref[x] = external
        t = x - (half - shared)
        if t >= 0:
            parcel_ref[t] = extra_ref[t]
            parcel_ref[shared + t] = density
            parcel_ref[2 * shared + t] = external


def exchange_lda(external, density):
    return external - slater * jnp.exp(jnp.log(density) * (1.0 / 3.0))


def potential_kernel(dens_ref, extp_ref, came_ref, pot_ref):
    for x in range(pot_ref.shape[0]):
        pot_ref[x] = exchange_lda(extp_ref[x], dens_ref[x] + came_ref[x])


def owned_kernel(dens_ref, extp_ref, extra_ref, parcel_ref, pot_ref, mine_ref, theirs_ref, out_ref):
    half, _, z_cells = dens_ref.shape
    late, shared = pot_ref.shape[0], mine_ref.shape[0]
    own = lax.axis_index("band")
    for t in range(shared):
        mine_ref[t] = exchange_lda(extp_ref[late + t], dens_ref[late + t] + parcel_ref[t])
        theirs_ref[t] = exchange_lda(parcel_ref[2 * shared + t], parcel_ref[shared + t] + extra_ref[t])
    for x in range(half):
        first, second = x + half * own, x + half * (1 - own)
        value = pot_ref[x] if x < late else mine_ref[x - late]
        out_ref[first] = value[:, : z_cells // 2]
        out_ref[second] = value[:, z_cells // 2 :]


def x_border_kernel(x_cells, y_cells, mate, inner_ref, face_ref, acc_ref):
    odd = lax.axis_index("dx") % 2
    upper = 1 - odd if mate else odd
    for b in range(inner_ref.shape[0] // (x_cells * y_cells)):
        for k in range(reach):
            x = b * x_cells + k + upper * (x_cells - 1 - 2 * k)
            here = pl.ds(pl.multiple_of(x * y_cells, 8), y_cells)
            total = inner_ref[here, :]
            for offset in range(k + 1, reach + 1):
                m = offset - 1 - k
                row = (reach - 1 - m + upper * (2 * m + 1 - reach)) * y_cells
                total = total + scaled[offset] * face_ref[b, pl.ds(pl.multiple_of(row, 8), y_cells), :]
            acc_ref[here, :] = total


def y_border_kernel(x_cells, y_cells, mate_ref, cross_ref, matrix_ref, inner_ref, acc_ref):
    odd = lax.axis_index("dy") % 2
    for face_ref, upper in ((mate_ref, 0), (cross_ref, 1)):
        matrix = matrix_ref[upper]
        for first in range(0, face_ref.shape[1], 8):
            block = jnp.concatenate([face_ref[i, pl.ds(first, 8), :] for i in range(reach)], axis=0)
            coarse = block.astype(jnp.bfloat16)
            fine = (block - coarse.astype(jnp.float32)).astype(jnp.bfloat16)
            added = jnp.dot(
                matrix, jnp.concatenate([coarse, fine, coarse], axis=0), preferred_element_type=jnp.float32
            )
            for line in range(8):
                row = (first + line) * y_cells + upper * (y_cells - 8)
                here = pl.ds(pl.multiple_of(row, 8), 8)
                acc_ref[here, :] = inner_ref[here, :] + added[8 * line : 8 * line + 8]


def final_kernel(
    x_cells, y_cells, orb_ref, acc_ref, mine_ref, theirs_ref, late_mine_ref, came_ref, out_ref, held_ref, sems
):
    z_cells = orb_ref.shape[1]
    bands = orb_ref.shape[0] // (x_cells * y_cells)
    own = own_lanes((y_cells, z_cells))
    half, part, late = x_cells // 2, x_cells // 8, came_ref.shape[0]
    copies = []
    for x in range(half):
        if x < late:
            mine, came = late_mine_ref[x], came_ref[x]
        else:
            mine, came = mine_ref[x - late], theirs_ref[x - late]
        near = jnp.where(own, mine, came)
        far = pltpu.roll(jnp.where(own, came, mine), z_cells // 2, 1)
        for t, potential in ((x, near), (x + half, far)):
            for b in range(bands):
                here = pl.ds((b * x_cells + t) * y_cells, y_cells)
                held_ref[here, :] = acc_ref[here, :] + potential * orb_ref[here, :]
        if x % part == part - 1:
            for first in (x + 1 - part, x + 1 - part + half):
                for b in range(bands):
                    piece = pl.ds((b * x_cells + first) * y_cells, part * y_cells)
                    copy = pltpu.make_async_copy(
                        held_ref.at[piece, :], out_ref.at[piece, :], sems.at[len(copies)]
                    )
                    copy.start()
                    copies.append(copy)
    for copy in copies:
        copy.wait()


def whole_kernel(orb_ref, acc_ref, potential_ref, out_ref):
    planes, y_cells, _ = potential_ref.shape
    for line in range(orb_ref.shape[0] // y_cells):
        here = pl.ds(line * y_cells, y_cells)
        out_ref[here, :] = acc_ref[here, :] + potential_ref[line % planes] * orb_ref[here, :]


def band_matrix(size, extent, periodic):
    matrix = np.zeros((size, size), np.float32)
    for i in range(size):
        group = i // extent * extent
        for offset in range(-reach, reach + 1):
            j = i - group + offset
            if periodic:
                j %= extent
            if 0 <= j < extent:
                matrix[i, group + j] += scaled[abs(offset)]
    return matrix


def face_matrix(upper):
    matrix = np.zeros((8, 8, reach, 8), np.float32)
    for k in range(reach):
        for offset in range(k + 1, reach + 1):
            m = offset - 1 - k
            line, source = (7 - k, m) if upper else (k, reach - 1 - m)
            for plane in range(8):
                matrix[plane, line, source, plane] = scaled[offset]
    return matrix.reshape(64, 8 * reach)


def split_constant(matrix):
    coarse = matrix.astype(jnp.bfloat16)
    return coarse, (matrix - coarse.astype(np.float32)).astype(jnp.bfloat16)


def call(kernel, outs, args, spaces=None, out_spaces=None, scratch=(), flops=1 << 20, aliases=None):
    shapes = [jax.ShapeDtypeStruct(shape, jnp.float32) for shape in outs]
    spaces = spaces or [pltpu.VMEM] * len(args)
    out_spaces = out_spaces or [pltpu.VMEM] * len(outs)
    return pl.pallas_call(
        kernel,
        out_shape=shapes,
        in_specs=[pl.BlockSpec(memory_space=space) for space in spaces],
        out_specs=[pl.BlockSpec(memory_space=space) for space in out_spaces],
        scratch_shapes=list(scratch),
        input_output_aliases=aliases or {},
        cost_estimate=pl.CostEstimate(flops=flops, bytes_accessed=0, transcendentals=0),
        compiler_params=pltpu.CompilerParams(vmem_limit_bytes=16 << 20),
    )(*args)


def on_device(orbitals, occupations, core_density, external):
    bands, x_cells, y_cells, z_cells = orbitals.shape
    rows = bands * x_cells * y_cells
    orb = pltpu.with_memory_space_constraint(orbitals.reshape(rows, z_cells), pltpu.HBM)
    flat = (rows, z_cells)
    y_halo = (reach, bands * x_cells, z_cells)
    x_halo = (bands, reach * y_cells, z_cells)
    bind = lambda kernel: functools.partial(kernel, x_cells, y_cells)
    paired = lax.axis_size("band") == 2
    if paired:
        half = x_cells // 2
        shared = half * 3 // 16
        late = half - shared
        planes = lambda count: (count, y_cells, z_cells)
        orb, keep, send, extra = call(
            bind(density_kernel),
            [flat, planes(half), planes(late), planes(shared)],
            [pltpu.with_memory_space_constraint(occupations, pltpu.HBM), orb],
            spaces=[pltpu.HBM, pltpu.HBM],
            scratch=[
                pltpu.SMEM(occupations.shape, jnp.float32),
                pltpu.SemaphoreType.DMA,
                pltpu.SemaphoreType.DMA((8 * bands,)),
            ],
        )
        came = exchanged(send, "band", 0)
    y_mate, y_cross, mate, cross = call(
        bind(halo_kernel), [y_halo, y_halo, x_halo, x_halo], [orb]
    )
    y_mate, y_cross = shifted(y_mate, "dy", True), shifted(y_cross, "dy", False)
    cross = exchanged(cross, "dx", 1)
    if paired:
        dens, extp, parcel = call(
            base_kernel,
            [planes(half), planes(half), planes(3 * shared)],
            [keep, extra, core_density, external],
        )
        parcel = exchanged(parcel, "band", 0)
        (late_mine,) = call(potential_kernel, [planes(late)], [dens, extp, came])
        came = exchanged(late_mine, "band", 0)
        orb, late_mine = lax.optimization_barrier((orb, late_mine))
    else:
        own_density = jnp.sum(occupations[:, None, None, None] * orbitals * orbitals, axis=0)
        total = lax.psum_scatter(own_density, "band", scatter_dimension=2, tiled=True)
        owned = external - slater * (total + core_density) ** (1.0 / 3.0)
        potential = lax.all_gather(owned, "band", axis=2, tiled=True)
    tile = 8 * y_cells
    middle = np.float32(scaled[0]) * np.eye(tile, dtype=np.float32)
    coarse, fine = split_constant(band_matrix(tile, y_cells, False) + middle)
    ymat = np.concatenate([coarse, fine], axis=0)
    coarse, fine = split_constant(band_matrix(z_cells, z_cells, True))
    zmat = np.block([[coarse, fine], [coarse, np.zeros_like(fine)]])
    (acc,) = call(
        bind(stencil_kernel), [flat], [orb, jnp.asarray(ymat), jnp.asarray(zmat)], flops=1 << 28
    )
    acc, mate = lax.optimization_barrier((acc, mate))
    mate = exchanged(mate, "dx", 0)
    if paired:
        acc, dens = lax.optimization_barrier((acc, dens))
        mine, theirs, owned = call(
            owned_kernel,
            [planes(shared), planes(shared), core_density.shape],
            [dens, extp, extra, parcel, late_mine],
        )
        acc, owned = lax.optimization_barrier((acc, owned))
    border = lambda which: functools.partial(x_border_kernel, x_cells, y_cells, which)
    sides = []
    for upper in (False, True):
        coarse, fine = split_constant(face_matrix(upper))
        sides.append(np.concatenate([coarse, coarse, fine], axis=1))
    (acc,) = call(
        bind(y_border_kernel), [flat], [y_mate, y_cross, jnp.asarray(np.stack(sides)), acc], aliases={3: 0}, flops=FY
    )
    (acc,) = call(border(False), [flat], [acc, cross], aliases={0: 0}, flops=FX)
    (acc,) = call(border(True), [flat], [acc, mate], aliases={0: 0}, flops=FM)
    if paired:
        (applied,) = call(
            bind(final_kernel),
            [flat],
            [orb, acc, mine, theirs, late_mine, came],
            out_spaces=[pltpu.HBM],
            scratch=[pltpu.VMEM(flat, jnp.float32), pltpu.SemaphoreType.DMA((8 * bands,))],
        )
    else:
        (applied,) = call(whole_kernel, [flat], [orb, acc, potential])
    return applied.reshape(orbitals.shape), owned


def solution(mesh):
    return jax.shard_map(
        on_device,
        mesh=mesh,
        in_specs=(
            P("band", "dx", "dy", None),
            P("band"),
            P("dx", "dy", "band"),
            P("dx", "dy", "band"),
        ),
        out_specs=(P("band", "dx", "dy", None), P("dx", "dy", "band")),
        check_vma=False,
    )
```

```python
import functools
import math

import jax
import jax.numpy as jnp
import numpy as np
from jax import lax
from jax.experimental import pallas as pl
from jax.experimental.pallas import tpu as pltpu
from jax.sharding import PartitionSpec as P

coeffs = (
    -5369.0 / 1800.0,
    12.0 / 7.0,
    -15.0 / 56.0,
    10.0 / 189.0,
    -1.0 / 112.0,
    2.0 / 1925.0,
    -1.0 / 16632.0,
)
reach = len(coeffs) - 1
FY, FX, FM = 1 << 20, 1 << 30, 0
grid_step = 2.0
slater = (3.0 / math.pi) ** (1.0 / 3.0)
scaled = tuple(-0.5 * c / (grid_step * grid_step) for c in coeffs)


def exchanged(block, axis, first):
    count = lax.axis_size(axis)
    pairs = [((first + i) % count, (first + (i ^ 1)) % count) for i in range(count)]
    return lax.ppermute(block, axis, pairs)


def shifted(block, axis, up):
    count = lax.axis_size(axis)
    pairs = [(i, (i + 1) % count) if up else ((i + 1) % count, i) for i in range(count)]
    return lax.ppermute(block, axis, pairs)


def own_lanes(shape):
    lane = lax.broadcasted_iota(jnp.int32, shape, 1)
    return (lane < shape[1] // 2) == (lax.axis_index("band") == 0)


def density_kernel(
    x_cells, y_cells, occ_ref, source_ref, orb_ref, keep_ref, send_ref, extra_ref, weight_ref, weight_sem, sems
):
    rows, z_cells = orb_ref.shape
    bands, half = rows // (x_cells * y_cells), x_cells // 2
    group = half // 4
    weights = pltpu.make_async_copy(occ_ref, weight_ref, weight_sem)
    weights.start()
    copies = []
    for part in range(4):
        for b in range(bands):
            for first in (part * group, part * group + half):
                piece = pl.ds((b * x_cells + first) * y_cells, group * y_cells)
                copies.append(
                    pltpu.make_async_copy(source_ref.at[piece, :], orb_ref.at[piece, :], sems.at[len(copies)])
                )
                copies[-1].start()
    own = own_lanes((y_cells, z_cells))

    def summed(x):
        total = None
        for b in range(bands):
            value = orb_ref[pl.ds((b * x_cells + x) * y_cells, y_cells), :]
            term = weight_ref[b] * value * value
            total = term if total is None else total + term
        return total

    weights.wait()
    late = send_ref.shape[0]
    for part in range(4):
        for copy in copies[2 * bands * part : 2 * bands * (part + 1)]:
            copy.wait()
        for x in range(part * group, (part + 1) * group):
            near = summed(x)
            far = pltpu.roll(summed(x + half), z_cells // 2, 1)
            keep_ref[x] = jnp.where(own, near, far)
            other = jnp.where(own, far, near)
            if x < late:
                send_ref[x] = other
            else:
                extra_ref[x - late] = other


def halo_kernel(x_cells, y_cells, orb_ref, y_mate_ref, y_cross_ref, x_mate_ref, x_cross_ref):
    lines = orb_ref.shape[0] // y_cells
    odd = lax.axis_index("dy") % 2
    high = y_cells - reach
    for i in range(reach):
        y_mate_ref[i] = orb_ref[pl.ds(high + i, lines, stride=y_cells), :]
        y_cross_ref[i] = orb_ref[pl.ds(i, lines, stride=y_cells), :]
    odd = lax.axis_index("dx") % 2
    high = (x_cells - reach) * y_cells
    for b in range(lines // x_cells):
        base = b * x_cells * y_cells
        x_mate_ref[b] = orb_ref[pl.ds(pl.multiple_of(base + (1 - odd) * high, 8), reach * y_cells), :]
        x_cross_ref[b] = orb_ref[pl.ds(pl.multiple_of(base + odd * high, 8), reach * y_cells), :]


def stencil_kernel(x_cells, y_cells, orb_ref, ymat_ref, zmat_ref, acc_ref):
    rows, z_cells = orb_ref.shape
    tile = ymat_ref.shape[1]
    for start in range(0, rows, tile):
        block = orb_ref[pl.ds(start, tile), :]
        coarse = block.astype(jnp.bfloat16)
        fine = (block - coarse.astype(jnp.float32)).astype(jnp.bfloat16)
        both = jnp.concatenate([coarse, fine], axis=1)
        along_z = jnp.dot(both, zmat_ref[...], preferred_element_type=jnp.float32)
        along_y = jnp.dot(ymat_ref[...], both, preferred_element_type=jnp.float32)
        acc_ref[pl.ds(start, tile), :] = (
            (along_z[:, :z_cells] + along_y[:tile, :z_cells])
            + (along_z[:, z_cells:] + along_y[:tile, z_cells:])
            + along_y[tile:, :z_cells]
        )
    for b in range(rows // (x_cells * y_cells)):
        for y in range(0, y_cells, 8):
            column = [orb_ref[pl.ds((b * x_cells + x) * y_cells + y, 8), :] for x in range(x_cells)]
            for x in range(x_cells):
                here = pl.ds((b * x_cells + x) * y_cells + y, 8)
                total = acc_ref[here, :]
                for offset in range(1, reach + 1):
                    pair = [column[t] for t in (x - offset, x + offset) if 0 <= t < x_cells]
                    total = total + scaled[offset] * sum(pair[1:], pair[0])
                acc_ref[here, :] = total


def base_kernel(keep_ref, extra_ref, core_ref, ext_ref, dens_ref, extp_ref, parcel_ref):
    half, shared = keep_ref.shape[0], extra_ref.shape[0]
    own = lax.axis_index("band")
    for x in range(half):
        first, second = x + half * own, x + half * (1 - own)
        density = keep_ref[x] + jnp.concatenate([core_ref[first], core_ref[second]], axis=1)
        external = jnp.concatenate([ext_ref[first], ext_ref[second]], axis=1)
        dens_ref[x] = density
        extp_ref[x] = external
        t = x - (half - shared)
        if t >= 0:
            parcel_ref[t] = extra_ref[t]
            parcel_ref[shared + t] = density
            parcel_ref[2 * shared + t] = external


def exchange_lda(external, density):
    return external - slater * jnp.exp(jnp.log(density) * (1.0 / 3.0))


def potential_kernel(dens_ref, extp_ref, came_ref, pot_ref):
    for x in range(pot_ref.shape[0]):
        pot_ref[x] = exchange_lda(extp_ref[x], dens_ref[x] + came_ref[x])


def owned_kernel(dens_ref, extp_ref, extra_ref, parcel_ref, pot_ref, mine_ref, theirs_ref, out_ref):
    half, _, z_cells = dens_ref.shape
    late, shared = pot_ref.shape[0], mine_ref.shape[0]
    own = lax.axis_index("band")
    for t in range(shared):
        mine_ref[t] = exchange_lda(extp_ref[late + t], dens_ref[late + t] + parcel_ref[t])
        theirs_ref[t] = exchange_lda(parcel_ref[2 * shared + t], parcel_ref[shared + t] + extra_ref[t])
    for x in range(half):
        first, second = x + half * own, x + half * (1 - own)
        value = pot_ref[x] if x < late else mine_ref[x - late]
        out_ref[first] = value[:, : z_cells // 2]
        out_ref[second] = value[:, z_cells // 2 :]


def copy_rows(from_ref, to_ref):
    for start in range(0, from_ref.shape[0], 256):
        to_ref[pl.ds(start, 256), :] = from_ref[pl.ds(start, 256), :]


def x_border_kernel(x_cells, y_cells, mate, inner_ref, face_ref, acc_ref):
    copy_rows(inner_ref, acc_ref)
    odd = lax.axis_index("dx") % 2
    upper = 1 - odd if mate else odd
    for b in range(inner_ref.shape[0] // (x_cells * y_cells)):
        for k in range(reach):
            x = b * x_cells + k + upper * (x_cells - 1 - 2 * k)
            here = pl.ds(pl.multiple_of(x * y_cells, 8), y_cells)
            total = inner_ref[here, :]
            for offset in range(k + 1, reach + 1):
                m = offset - 1 - k
                row = (reach - 1 - m + upper * (2 * m + 1 - reach)) * y_cells
                total = total + scaled[offset] * face_ref[b, pl.ds(pl.multiple_of(row, 8), y_cells), :]
            acc_ref[here, :] = total


def y_border_kernel(x_cells, y_cells, mate_ref, cross_ref, matrix_ref, inner_ref, acc_ref):
    copy_rows(inner_ref, acc_ref)
    odd = lax.axis_index("dy") % 2
    for face_ref, upper in ((mate_ref, 0), (cross_ref, 1)):
        matrix = matrix_ref[upper]
        for first in range(0, face_ref.shape[1], 8):
            block = jnp.concatenate([face_ref[i, pl.ds(first, 8), :] for i in range(reach)], axis=0)
            coarse = block.astype(jnp.bfloat16)
            fine = (block - coarse.astype(jnp.float32)).astype(jnp.bfloat16)
            added = jnp.dot(
                matrix, jnp.concatenate([coarse, fine, coarse], axis=0), preferred_element_type=jnp.float32
            )
            for line in range(8):
                row = (first + line) * y_cells + upper * (y_cells - 8)
                here = pl.ds(pl.multiple_of(row, 8), 8)
                acc_ref[here, :] = inner_ref[here, :] + added[8 * line : 8 * line + 8]


def final_kernel(
    x_cells, y_cells, orb_ref, acc_ref, mine_ref, theirs_ref, late_mine_ref, came_ref, out_ref, held_ref, sems
):
    z_cells = orb_ref.shape[1]
    bands = orb_ref.shape[0] // (x_cells * y_cells)
    own = own_lanes((y_cells, z_cells))
    half, part, late = x_cells // 2, x_cells // 8, came_ref.shape[0]
    copies = []
    for x in range(half):
        if x < late:
            mine, came = late_mine_ref[x], came_ref[x]
        else:
            mine, came = mine_ref[x - late], theirs_ref[x - late]
        near = jnp.where(own, mine, came)
        far = pltpu.roll(jnp.where(own, came, mine), z_cells // 2, 1)
        for t, potential in ((x, near), (x + half, far)):
            for b in range(bands):
                here = pl.ds((b * x_cells + t) * y_cells, y_cells)
                held_ref[here, :] = acc_ref[here, :] + potential * orb_ref[here, :]
        if x % part == part - 1:
            for first in (x + 1 - part, x + 1 - part + half):
                for b in range(bands):
                    piece = pl.ds((b * x_cells + first) * y_cells, part * y_cells)
                    copy = pltpu.make_async_copy(
                        held_ref.at[piece, :], out_ref.at[piece, :], sems.at[len(copies)]
                    )
                    copy.start()
                    copies.append(copy)
    for copy in copies:
        copy.wait()


def whole_kernel(orb_ref, acc_ref, potential_ref, out_ref):
    planes, y_cells, _ = potential_ref.shape
    for line in range(orb_ref.shape[0] // y_cells):
        here = pl.ds(line * y_cells, y_cells)
        out_ref[here, :] = acc_ref[here, :] + potential_ref[line % planes] * orb_ref[here, :]


def band_matrix(size, extent, periodic):
    matrix = np.zeros((size, size), np.float32)
    for i in range(size):
        group = i // extent * extent
        for offset in range(-reach, reach + 1):
            j = i - group + offset
            if periodic:
                j %= extent
            if 0 <= j < extent:
                matrix[i, group + j] += scaled[abs(offset)]
    return matrix


def face_matrix(upper):
    matrix = np.zeros((8, 8, reach, 8), np.float32)
    for k in range(reach):
        for offset in range(k + 1, reach + 1):
            m = offset - 1 - k
            line, source = (7 - k, m) if upper else (k, reach - 1 - m)
            for plane in range(8):
                matrix[plane, line, source, plane] = scaled[offset]
    return matrix.reshape(64, 8 * reach)


def split_constant(matrix):
    coarse = matrix.astype(jnp.bfloat16)
    return coarse, (matrix - coarse.astype(np.float32)).astype(jnp.bfloat16)


def call(kernel, outs, args, spaces=None, out_spaces=None, scratch=(), flops=1 << 20, aliases=None):
    shapes = [jax.ShapeDtypeStruct(shape, jnp.float32) for shape in outs]
    spaces = spaces or [pltpu.VMEM] * len(args)
    out_spaces = out_spaces or [pltpu.VMEM] * len(outs)
    return pl.pallas_call(
        kernel,
        out_shape=shapes,
        in_specs=[pl.BlockSpec(memory_space=space) for space in spaces],
        out_specs=[pl.BlockSpec(memory_space=space) for space in out_spaces],
        scratch_shapes=list(scratch),
        input_output_aliases=aliases or {},
        cost_estimate=pl.CostEstimate(flops=flops, bytes_accessed=0, transcendentals=0),
        compiler_params=pltpu.CompilerParams(vmem_limit_bytes=16 << 20),
    )(*args)


def on_device(orbitals, occupations, core_density, external):
    bands, x_cells, y_cells, z_cells = orbitals.shape
    rows = bands * x_cells * y_cells
    orb = pltpu.with_memory_space_constraint(orbitals.reshape(rows, z_cells), pltpu.HBM)
    flat = (rows, z_cells)
    y_halo = (reach, bands * x_cells, z_cells)
    x_halo = (bands, reach * y_cells, z_cells)
    bind = lambda kernel: functools.partial(kernel, x_cells, y_cells)
    paired = lax.axis_size("band") == 2
    if paired:
        half = x_cells // 2
        shared = half * 3 // 16
        late = half - shared
        planes = lambda count: (count, y_cells, z_cells)
        orb, keep, send, extra = call(
            bind(density_kernel),
            [flat, planes(half), planes(late), planes(shared)],
            [pltpu.with_memory_space_constraint(occupations, pltpu.HBM), orb],
            spaces=[pltpu.HBM, pltpu.HBM],
            scratch=[
                pltpu.SMEM(occupations.shape, jnp.float32),
                pltpu.SemaphoreType.DMA,
                pltpu.SemaphoreType.DMA((8 * bands,)),
            ],
        )
        came = exchanged(send, "band", 0)
    y_mate, y_cross, mate, cross = call(
        bind(halo_kernel), [y_halo, y_halo, x_halo, x_halo], [orb]
    )
    y_mate, y_cross = shifted(y_mate, "dy", True), shifted(y_cross, "dy", False)
    cross = exchanged(cross, "dx", 1)
    if paired:
        dens, extp, parcel = call(
            base_kernel,
            [planes(half), planes(half), planes(3 * shared)],
            [keep, extra, core_density, external],
        )
        parcel = exchanged(parcel, "band", 0)
        (late_mine,) = call(potential_kernel, [planes(late)], [dens, extp, came])
        came = exchanged(late_mine, "band", 0)
        orb, late_mine = lax.optimization_barrier((orb, late_mine))
    else:
        own_density = jnp.sum(occupations[:, None, None, None] * orbitals * orbitals, axis=0)
        total = lax.psum_scatter(own_density, "band", scatter_dimension=2, tiled=True)
        owned = external - slater * (total + core_density) ** (1.0 / 3.0)
        potential = lax.all_gather(owned, "band", axis=2, tiled=True)
    tile = 8 * y_cells
    middle = np.float32(scaled[0]) * np.eye(tile, dtype=np.float32)
    coarse, fine = split_constant(band_matrix(tile, y_cells, False) + middle)
    ymat = np.concatenate([coarse, fine], axis=0)
    coarse, fine = split_constant(band_matrix(z_cells, z_cells, True))
    zmat = np.block([[coarse, fine], [coarse, np.zeros_like(fine)]])
    (acc,) = call(
        bind(stencil_kernel), [flat], [orb, jnp.asarray(ymat), jnp.asarray(zmat)], flops=1 << 28
    )
    acc, mate = lax.optimization_barrier((acc, mate))
    mate = exchanged(mate, "dx", 0)
    if paired:
        acc, dens = lax.optimization_barrier((acc, dens))
        mine, theirs, owned = call(
            owned_kernel,
            [planes(shared), planes(shared), core_density.shape],
            [dens, extp, extra, parcel, late_mine],
        )
        acc, owned = lax.optimization_barrier((acc, owned))
    border = lambda which: functools.partial(x_border_kernel, x_cells, y_cells, which)
    sides = []
    for upper in (False, True):
        coarse, fine = split_constant(face_matrix(upper))
        sides.append(np.concatenate([coarse, coarse, fine], axis=1))
    (acc,) = call(
        bind(y_border_kernel), [flat], [y_mate, y_cross, jnp.asarray(np.stack(sides)), acc], aliases={3: 0}, flops=FY
    )
    (acc,) = call(border(False), [flat], [acc, cross], aliases={0: 0}, flops=FX)
    (acc,) = call(border(True), [flat], [acc, mate], aliases={0: 0}, flops=FM)
    if paired:
        (applied,) = call(
            bind(final_kernel),
            [flat],
            [orb, acc, mine, theirs, late_mine, came],
            out_spaces=[pltpu.HBM],
            scratch=[pltpu.VMEM(flat, jnp.float32), pltpu.SemaphoreType.DMA((8 * bands,))],
        )
    else:
        (applied,) = call(whole_kernel, [flat], [orb, acc, potential])
    return applied.reshape(orbitals.shape), owned


def solution(mesh):
    return jax.shard_map(
        on_device,
        mesh=mesh,
        in_specs=(
            P("band", "dx", "dy", None),
            P("band"),
            P("dx", "dy", "band"),
            P("dx", "dy", "band"),
        ),
        out_specs=(P("band", "dx", "dy", None), P("dx", "dy", "band")),
        check_vma=False,
    )
```

```python
import functools
import math

import jax
import jax.numpy as jnp
import numpy as np
from jax import lax
from jax.experimental import pallas as pl
from jax.experimental.pallas import tpu as pltpu
from jax.sharding import PartitionSpec as P

coeffs = (
    -5369.0 / 1800.0,
    12.0 / 7.0,
    -15.0 / 56.0,
    10.0 / 189.0,
    -1.0 / 112.0,
    2.0 / 1925.0,
    -1.0 / 16632.0,
)
reach = len(coeffs) - 1
FY, FX, FM = 1 << 20, 1 << 30, 0
grid_step = 2.0
slater = (3.0 / math.pi) ** (1.0 / 3.0)
scaled = tuple(-0.5 * c / (grid_step * grid_step) for c in coeffs)


def exchanged(block, axis, first):
    count = lax.axis_size(axis)
    pairs = [((first + i) % count, (first + (i ^ 1)) % count) for i in range(count)]
    return lax.ppermute(block, axis, pairs)


def shifted(block, axis, up):
    count = lax.axis_size(axis)
    pairs = [(i, (i + 1) % count) if up else ((i + 1) % count, i) for i in range(count)]
    return lax.ppermute(block, axis, pairs)


def own_lanes(shape):
    lane = lax.broadcasted_iota(jnp.int32, shape, 1)
    return (lane < shape[1] // 2) == (lax.axis_index("band") == 0)


def density_kernel(
    x_cells, y_cells, occ_ref, source_ref, orb_ref, keep_ref, send_ref, extra_ref, weight_ref, weight_sem, sems
):
    rows, z_cells = orb_ref.shape
    bands, half = rows // (x_cells * y_cells), x_cells // 2
    group = half // 4
    weights = pltpu.make_async_copy(occ_ref, weight_ref, weight_sem)
    weights.start()
    copies = []
    for part in range(4):
        for b in range(bands):
            for first in (part * group, part * group + half):
                piece = pl.ds((b * x_cells + first) * y_cells, group * y_cells)
                copies.append(
                    pltpu.make_async_copy(source_ref.at[piece, :], orb_ref.at[piece, :], sems.at[len(copies)])
                )
                copies[-1].start()
    own = own_lanes((y_cells, z_cells))

    def summed(x):
        total = None
        for b in range(bands):
            value = orb_ref[pl.ds((b * x_cells + x) * y_cells, y_cells), :]
            term = weight_ref[b] * value * value
            total = term if total is None else total + term
        return total

    weights.wait()
    late = send_ref.shape[0]
    for part in range(4):
        for copy in copies[2 * bands * part : 2 * bands * (part + 1)]:
            copy.wait()
        for x in range(part * group, (part + 1) * group):
            near = summed(x)
            far = pltpu.roll(summed(x + half), z_cells // 2, 1)
            keep_ref[x] = jnp.where(own, near, far)
            other = jnp.where(own, far, near)
            if x < late:
                send_ref[x] = other
            else:
                extra_ref[x - late] = other


def halo_kernel(x_cells, y_cells, orb_ref, y_mate_ref, y_cross_ref, x_mate_ref, x_cross_ref):
    lines = orb_ref.shape[0] // y_cells
    odd = lax.axis_index("dy") % 2
    high = y_cells - reach
    for i in range(reach):
        y_mate_ref[i] = orb_ref[pl.ds(high + i, lines, stride=y_cells), :]
        y_cross_ref[i] = orb_ref[pl.ds(i, lines, stride=y_cells), :]
    odd = lax.axis_index("dx") % 2
    high = (x_cells - reach) * y_cells
    for b in range(lines // x_cells):
        base = b * x_cells * y_cells
        x_mate_ref[b] = orb_ref[pl.ds(pl.multiple_of(base + (1 - odd) * high, 8), reach * y_cells), :]
        x_cross_ref[b] = orb_ref[pl.ds(pl.multiple_of(base + odd * high, 8), reach * y_cells), :]


def stencil_kernel(x_cells, y_cells, orb_ref, ymat_ref, zmat_ref, acc_ref):
    rows, z_cells = orb_ref.shape
    tile = ymat_ref.shape[1]
    for start in range(0, rows, tile):
        block = orb_ref[pl.ds(start, tile), :]
        coarse = block.astype(jnp.bfloat16)
        fine = (block - coarse.astype(jnp.float32)).astype(jnp.bfloat16)
        both = jnp.concatenate([coarse, fine], axis=1)
        along_z = jnp.dot(both, zmat_ref[...], preferred_element_type=jnp.float32)
        along_y = jnp.dot(ymat_ref[...], both, preferred_element_type=jnp.float32)
        acc_ref[pl.ds(start, tile), :] = (
            (along_z[:, :z_cells] + along_y[:tile, :z_cells])
            + (along_z[:, z_cells:] + along_y[:tile, z_cells:])
            + along_y[tile:, :z_cells]
        )
    for b in range(rows // (x_cells * y_cells)):
        for y in range(0, y_cells, 8):
            column = [orb_ref[pl.ds((b * x_cells + x) * y_cells + y, 8), :] for x in range(x_cells)]
            for x in range(x_cells):
                here = pl.ds((b * x_cells + x) * y_cells + y, 8)
                total = acc_ref[here, :]
                for offset in range(1, reach + 1):
                    pair = [column[t] for t in (x - offset, x + offset) if 0 <= t < x_cells]
                    total = total + scaled[offset] * sum(pair[1:], pair[0])
                acc_ref[here, :] = total


def base_kernel(keep_ref, extra_ref, core_ref, ext_ref, dens_ref, extp_ref, parcel_ref):
    half, shared = keep_ref.shape[0], extra_ref.shape[0]
    own = lax.axis_index("band")
    for x in range(half):
        first, second = x + half * own, x + half * (1 - own)
        density = keep_ref[x] + jnp.concatenate([core_ref[first], core_ref[second]], axis=1)
        external = jnp.concatenate([ext_ref[first], ext_ref[second]], axis=1)
        dens_ref[x] = density
        extp_ref[x] = external
        t = x - (half - shared)
        if t >= 0:
            parcel_ref[t] = extra_ref[t]
            parcel_ref[shared + t] = density
            parcel_ref[2 * shared + t] = external


def exchange_lda(external, density):
    return external - slater * jnp.exp(jnp.log(density) * (1.0 / 3.0))


def potential_kernel(dens_ref, extp_ref, came_ref, pot_ref):
    for x in range(pot_ref.shape[0]):
        pot_ref[x] = exchange_lda(extp_ref[x], dens_ref[x] + came_ref[x])


def owned_kernel(dens_ref, extp_ref, extra_ref, parcel_ref, pot_ref, mine_ref, theirs_ref, out_ref):
    half, _, z_cells = dens_ref.shape
    late, shared = pot_ref.shape[0], mine_ref.shape[0]
    own = lax.axis_index("band")
    for t in range(shared):
        mine_ref[t] = exchange_lda(extp_ref[late + t], dens_ref[late + t] + parcel_ref[t])
        theirs_ref[t] = exchange_lda(parcel_ref[2 * shared + t], parcel_ref[shared + t] + extra_ref[t])
    for x in range(half):
        first, second = x + half * own, x + half * (1 - own)
        value = pot_ref[x] if x < late else mine_ref[x - late]
        out_ref[first] = value[:, : z_cells // 2]
        out_ref[second] = value[:, z_cells // 2 :]


def copy_rows(from_ref, to_ref):
    for start in range(0, from_ref.shape[0], 256):
        to_ref[pl.ds(start, 256), :] = from_ref[pl.ds(start, 256), :]


def x_border_kernel(x_cells, y_cells, mate, inner_ref, face_ref, acc_ref):
    copy_rows(inner_ref, acc_ref)
    odd = lax.axis_index("dx") % 2
    upper = 1 - odd if mate else odd
    for b in range(inner_ref.shape[0] // (x_cells * y_cells)):
        for k in range(reach):
            x = b * x_cells + k + upper * (x_cells - 1 - 2 * k)
            here = pl.ds(pl.multiple_of(x * y_cells, 8), y_cells)
            total = inner_ref[here, :]
            for offset in range(k + 1, reach + 1):
                m = offset - 1 - k
                row = (reach - 1 - m + upper * (2 * m + 1 - reach)) * y_cells
                total = total + scaled[offset] * face_ref[b, pl.ds(pl.multiple_of(row, 8), y_cells), :]
            acc_ref[here, :] = total


def y_border_kernel(x_cells, y_cells, mate_ref, cross_ref, matrix_ref, inner_ref, acc_ref):
    copy_rows(inner_ref, acc_ref)
    odd = lax.axis_index("dy") % 2
    for face_ref, upper in ((mate_ref, 0), (cross_ref, 1)):
        matrix = matrix_ref[upper]
        for first in range(0, face_ref.shape[1], 8):
            block = jnp.concatenate([face_ref[i, pl.ds(first, 8), :] for i in range(reach)], axis=0)
            coarse = block.astype(jnp.bfloat16)
            fine = (block - coarse.astype(jnp.float32)).astype(jnp.bfloat16)
            added = jnp.dot(
                matrix, jnp.concatenate([coarse, fine, coarse], axis=0), preferred_element_type=jnp.float32
            )
            for line in range(8):
                row = (first + line) * y_cells + upper * (y_cells - 8)
                here = pl.ds(pl.multiple_of(row, 8), 8)
                acc_ref[here, :] = inner_ref[here, :] + added[8 * line : 8 * line + 8]


def final_kernel(
    x_cells, y_cells, orb_ref, acc_ref, mine_ref, theirs_ref, late_mine_ref, came_ref, out_ref, held_ref, sems
):
    z_cells = orb_ref.shape[1]
    bands = orb_ref.shape[0] // (x_cells * y_cells)
    own = own_lanes((y_cells, z_cells))
    half, part, late = x_cells // 2, x_cells // 4, came_ref.shape[0]
    copies = []
    for x in range(half):
        if x < late:
            mine, came = late_mine_ref[x], came_ref[x]
        else:
            mine, came = mine_ref[x - late], theirs_ref[x - late]
        near = jnp.where(own, mine, came)
        far = pltpu.roll(jnp.where(own, came, mine), z_cells // 2, 1)
        for t, potential in ((x, near), (x + half, far)):
            for b in range(bands):
                here = pl.ds((b * x_cells + t) * y_cells, y_cells)
                held_ref[here, :] = acc_ref[here, :] + potential * orb_ref[here, :]
        if x % part == part - 1:
            for first in (x + 1 - part, x + 1 - part + half):
                for b in range(bands):
                    piece = pl.ds((b * x_cells + first) * y_cells, part * y_cells)
                    copy = pltpu.make_async_copy(
                        held_ref.at[piece, :], out_ref.at[piece, :], sems.at[len(copies)]
                    )
                    copy.start()
                    copies.append(copy)
    for copy in copies:
        copy.wait()


def whole_kernel(orb_ref, acc_ref, potential_ref, out_ref):
    planes, y_cells, _ = potential_ref.shape
    for line in range(orb_ref.shape[0] // y_cells):
        here = pl.ds(line * y_cells, y_cells)
        out_ref[here, :] = acc_ref[here, :] + potential_ref[line % planes] * orb_ref[here, :]


def band_matrix(size, extent, periodic):
    matrix = np.zeros((size, size), np.float32)
    for i in range(size):
        group = i // extent * extent
        for offset in range(-reach, reach + 1):
            j = i - group + offset
            if periodic:
                j %= extent
            if 0 <= j < extent:
                matrix[i, group + j] += scaled[abs(offset)]
    return matrix


def face_matrix(upper):
    matrix = np.zeros((8, 8, reach, 8), np.float32)
    for k in range(reach):
        for offset in range(k + 1, reach + 1):
            m = offset - 1 - k
            line, source = (7 - k, m) if upper else (k, reach - 1 - m)
            for plane in range(8):
                matrix[plane, line, source, plane] = scaled[offset]
    return matrix.reshape(64, 8 * reach)


def split_constant(matrix):
    coarse = matrix.astype(jnp.bfloat16)
    return coarse, (matrix - coarse.astype(np.float32)).astype(jnp.bfloat16)


def call(kernel, outs, args, spaces=None, out_spaces=None, scratch=(), flops=1 << 20, aliases=None):
    shapes = [jax.ShapeDtypeStruct(shape, jnp.float32) for shape in outs]
    spaces = spaces or [pltpu.VMEM] * len(args)
    out_spaces = out_spaces or [pltpu.VMEM] * len(outs)
    return pl.pallas_call(
        kernel,
        out_shape=shapes,
        in_specs=[pl.BlockSpec(memory_space=space) for space in spaces],
        out_specs=[pl.BlockSpec(memory_space=space) for space in out_spaces],
        scratch_shapes=list(scratch),
        input_output_aliases=aliases or {},
        cost_estimate=pl.CostEstimate(flops=flops, bytes_accessed=0, transcendentals=0),
        compiler_params=pltpu.CompilerParams(vmem_limit_bytes=16 << 20),
    )(*args)


def on_device(orbitals, occupations, core_density, external):
    bands, x_cells, y_cells, z_cells = orbitals.shape
    rows = bands * x_cells * y_cells
    orb = pltpu.with_memory_space_constraint(orbitals.reshape(rows, z_cells), pltpu.HBM)
    flat = (rows, z_cells)
    y_halo = (reach, bands * x_cells, z_cells)
    x_halo = (bands, reach * y_cells, z_cells)
    bind = lambda kernel: functools.partial(kernel, x_cells, y_cells)
    paired = lax.axis_size("band") == 2
    if paired:
        half = x_cells // 2
        shared = half * 3 // 16
        late = half - shared
        planes = lambda count: (count, y_cells, z_cells)
        orb, keep, send, extra = call(
            bind(density_kernel),
            [flat, planes(half), planes(late), planes(shared)],
            [pltpu.with_memory_space_constraint(occupations, pltpu.HBM), orb],
            spaces=[pltpu.HBM, pltpu.HBM],
            scratch=[
                pltpu.SMEM(occupations.shape, jnp.float32),
                pltpu.SemaphoreType.DMA,
                pltpu.SemaphoreType.DMA((8 * bands,)),
            ],
        )
        came = exchanged(send, "band", 0)
    y_mate, y_cross, mate, cross = call(
        bind(halo_kernel), [y_halo, y_halo, x_halo, x_halo], [orb]
    )
    y_mate, y_cross = shifted(y_mate, "dy", True), shifted(y_cross, "dy", False)
    cross = exchanged(cross, "dx", 1)
    if paired:
        dens, extp, parcel = call(
            base_kernel,
            [planes(half), planes(half), planes(3 * shared)],
            [keep, extra, core_density, external],
        )
        parcel = exchanged(parcel, "band", 0)
        (late_mine,) = call(potential_kernel, [planes(late)], [dens, extp, came])
        came = exchanged(late_mine, "band", 0)
        orb, late_mine = lax.optimization_barrier((orb, late_mine))
    else:
        own_density = jnp.sum(occupations[:, None, None, None] * orbitals * orbitals, axis=0)
        total = lax.psum_scatter(own_density, "band", scatter_dimension=2, tiled=True)
        owned = external - slater * (total + core_density) ** (1.0 / 3.0)
        potential = lax.all_gather(owned, "band", axis=2, tiled=True)
    tile = 8 * y_cells
    middle = np.float32(scaled[0]) * np.eye(tile, dtype=np.float32)
    coarse, fine = split_constant(band_matrix(tile, y_cells, False) + middle)
    ymat = np.concatenate([coarse, fine], axis=0)
    coarse, fine = split_constant(band_matrix(z_cells, z_cells, True))
    zmat = np.block([[coarse, fine], [coarse, np.zeros_like(fine)]])
    (acc,) = call(
        bind(stencil_kernel), [flat], [orb, jnp.asarray(ymat), jnp.asarray(zmat)], flops=1 << 28
    )
    acc, mate = lax.optimization_barrier((acc, mate))
    mate = exchanged(mate, "dx", 0)
    if paired:
        acc, dens = lax.optimization_barrier((acc, dens))
        mine, theirs, owned = call(
            owned_kernel,
            [planes(shared), planes(shared), core_density.shape],
            [dens, extp, extra, parcel, late_mine],
        )
        acc, owned = lax.optimization_barrier((acc, owned))
    border = lambda which: functools.partial(x_border_kernel, x_cells, y_cells, which)
    sides = []
    for upper in (False, True):
        coarse, fine = split_constant(face_matrix(upper))
        sides.append(np.concatenate([coarse, coarse, fine], axis=1))
    (acc,) = call(
        bind(y_border_kernel), [flat], [y_mate, y_cross, jnp.asarray(np.stack(sides)), acc], flops=FY
    )
    (acc,) = call(border(False), [flat], [acc, cross], flops=FX)
    (acc,) = call(border(True), [flat], [acc, mate], flops=FM)
    if paired:
        (applied,) = call(
            bind(final_kernel),
            [flat],
            [orb, acc, mine, theirs, late_mine, came],
            out_spaces=[pltpu.HBM],
            scratch=[pltpu.VMEM(flat, jnp.float32), pltpu.SemaphoreType.DMA((8 * bands,))],
        )
    else:
        (applied,) = call(whole_kernel, [flat], [orb, acc, potential])
    return applied.reshape(orbitals.shape), owned


def solution(mesh):
    return jax.shard_map(
        on_device,
        mesh=mesh,
        in_specs=(
            P("band", "dx", "dy", None),
            P("band"),
            P("dx", "dy", "band"),
            P("dx", "dy", "band"),
        ),
        out_specs=(P("band", "dx", "dy", None), P("dx", "dy", "band")),
        check_vma=False,
    )
```

```python
import functools
import math

import jax
import jax.numpy as jnp
import numpy as np
from jax import lax
from jax.experimental import pallas as pl
from jax.experimental.pallas import tpu as pltpu
from jax.sharding import PartitionSpec as P

coeffs = (
    -5369.0 / 1800.0,
    12.0 / 7.0,
    -15.0 / 56.0,
    10.0 / 189.0,
    -1.0 / 112.0,
    2.0 / 1925.0,
    -1.0 / 16632.0,
)
reach = len(coeffs) - 1
FY, FX, FM = 1 << 20, 1 << 30, 0
grid_step = 2.0
slater = (3.0 / math.pi) ** (1.0 / 3.0)
scaled = tuple(-0.5 * c / (grid_step * grid_step) for c in coeffs)


def exchanged(block, axis, first):
    count = lax.axis_size(axis)
    pairs = [((first + i) % count, (first + (i ^ 1)) % count) for i in range(count)]
    return lax.ppermute(block, axis, pairs)


def shifted(block, axis, up):
    count = lax.axis_size(axis)
    pairs = [(i, (i + 1) % count) if up else ((i + 1) % count, i) for i in range(count)]
    return lax.ppermute(block, axis, pairs)


def own_lanes(shape):
    lane = lax.broadcasted_iota(jnp.int32, shape, 1)
    return (lane < shape[1] // 2) == (lax.axis_index("band") == 0)


def density_kernel(
    x_cells, y_cells, occ_ref, source_ref, orb_ref, keep_ref, send_ref, extra_ref, weight_ref, weight_sem, sems
):
    rows, z_cells = orb_ref.shape
    bands, half = rows // (x_cells * y_cells), x_cells // 2
    group = half // 4
    weights = pltpu.make_async_copy(occ_ref, weight_ref, weight_sem)
    weights.start()
    copies = []
    for part in range(4):
        for b in range(bands):
            for first in (part * group, part * group + half):
                piece = pl.ds((b * x_cells + first) * y_cells, group * y_cells)
                copies.append(
                    pltpu.make_async_copy(source_ref.at[piece, :], orb_ref.at[piece, :], sems.at[len(copies)])
                )
                copies[-1].start()
    own = own_lanes((y_cells, z_cells))

    def summed(x):
        total = None
        for b in range(bands):
            value = orb_ref[pl.ds((b * x_cells + x) * y_cells, y_cells), :]
            term = weight_ref[b] * value * value
            total = term if total is None else total + term
        return total

    weights.wait()
    late = send_ref.shape[0]
    for part in range(4):
        for copy in copies[2 * bands * part : 2 * bands * (part + 1)]:
            copy.wait()
        for x in range(part * group, (part + 1) * group):
            near = summed(x)
            far = pltpu.roll(summed(x + half), z_cells // 2, 1)
            keep_ref[x] = jnp.where(own, near, far)
            other = jnp.where(own, far, near)
            if x < late:
                send_ref[x] = other
            else:
                extra_ref[x - late] = other


def halo_kernel(x_cells, y_cells, orb_ref, y_mate_ref, y_cross_ref, x_mate_ref, x_cross_ref):
    lines = orb_ref.shape[0] // y_cells
    odd = lax.axis_index("dy") % 2
    high = y_cells - reach
    for i in range(reach):
        y_mate_ref[i] = orb_ref[pl.ds(high + i, lines, stride=y_cells), :]
        y_cross_ref[i] = orb_ref[pl.ds(i, lines, stride=y_cells), :]
    odd = lax.axis_index("dx") % 2
    high = (x_cells - reach) * y_cells
    for b in range(lines // x_cells):
        base = b * x_cells * y_cells
        x_mate_ref[b] = orb_ref[pl.ds(pl.multiple_of(base + (1 - odd) * high, 8), reach * y_cells), :]
        x_cross_ref[b] = orb_ref[pl.ds(pl.multiple_of(base + odd * high, 8), reach * y_cells), :]


def stencil_kernel(x_cells, y_cells, orb_ref, ymat_ref, zmat_ref, acc_ref):
    rows, z_cells = orb_ref.shape
    tile = ymat_ref.shape[1]
    for start in range(0, rows, tile):
        block = orb_ref[pl.ds(start, tile), :]
        coarse = block.astype(jnp.bfloat16)
        fine = (block - coarse.astype(jnp.float32)).astype(jnp.bfloat16)
        both = jnp.concatenate([coarse, fine], axis=1)
        along_z = jnp.dot(both, zmat_ref[...], preferred_element_type=jnp.float32)
        along_y = jnp.dot(ymat_ref[...], both, preferred_element_type=jnp.float32)
        acc_ref[pl.ds(start, tile), :] = (
            (along_z[:, :z_cells] + along_y[:tile, :z_cells])
            + (along_z[:, z_cells:] + along_y[:tile, z_cells:])
            + along_y[tile:, :z_cells]
        )
    for b in range(rows // (x_cells * y_cells)):
        for y in range(0, y_cells, 8):
            column = [orb_ref[pl.ds((b * x_cells + x) * y_cells + y, 8), :] for x in range(x_cells)]
            for x in range(x_cells):
                here = pl.ds((b * x_cells + x) * y_cells + y, 8)
                total = acc_ref[here, :]
                for offset in range(1, reach + 1):
                    pair = [column[t] for t in (x - offset, x + offset) if 0 <= t < x_cells]
                    total = total + scaled[offset] * sum(pair[1:], pair[0])
                acc_ref[here, :] = total


def base_kernel(keep_ref, extra_ref, core_ref, ext_ref, dens_ref, extp_ref, parcel_ref):
    half, shared = keep_ref.shape[0], extra_ref.shape[0]
    own = lax.axis_index("band")
    for x in range(half):
        first, second = x + half * own, x + half * (1 - own)
        density = keep_ref[x] + jnp.concatenate([core_ref[first], core_ref[second]], axis=1)
        external = jnp.concatenate([ext_ref[first], ext_ref[second]], axis=1)
        dens_ref[x] = density
        extp_ref[x] = external
        t = x - (half - shared)
        if t >= 0:
            parcel_ref[t] = extra_ref[t]
            parcel_ref[shared + t] = density
            parcel_ref[2 * shared + t] = external


def exchange_lda(external, density):
    return external - slater * jnp.exp(jnp.log(density) * (1.0 / 3.0))


def potential_kernel(dens_ref, extp_ref, came_ref, pot_ref):
    for x in range(pot_ref.shape[0]):
        pot_ref[x] = exchange_lda(extp_ref[x], dens_ref[x] + came_ref[x])


def owned_kernel(dens_ref, extp_ref, extra_ref, parcel_ref, pot_ref, mine_ref, theirs_ref, out_ref):
    half, _, z_cells = dens_ref.shape
    late, shared = pot_ref.shape[0], mine_ref.shape[0]
    own = lax.axis_index("band")
    for t in range(shared):
        mine_ref[t] = exchange_lda(extp_ref[late + t], dens_ref[late + t] + parcel_ref[t])
        theirs_ref[t] = exchange_lda(parcel_ref[2 * shared + t], parcel_ref[shared + t] + extra_ref[t])
    for x in range(half):
        first, second = x + half * own, x + half * (1 - own)
        value = pot_ref[x] if x < late else mine_ref[x - late]
        out_ref[first] = value[:, : z_cells // 2]
        out_ref[second] = value[:, z_cells // 2 :]


def copy_rows(from_ref, to_ref):
    for start in range(0, from_ref.shape[0], 256):
        to_ref[pl.ds(start, 256), :] = from_ref[pl.ds(start, 256), :]


def x_border_kernel(x_cells, y_cells, mate, inner_ref, face_ref, acc_ref):
    copy_rows(inner_ref, acc_ref)
    odd = lax.axis_index("dx") % 2
    upper = 1 - odd if mate else odd
    for b in range(inner_ref.shape[0] // (x_cells * y_cells)):
        for k in range(reach):
            x = b * x_cells + k + upper * (x_cells - 1 - 2 * k)
            here = pl.ds(pl.multiple_of(x * y_cells, 8), y_cells)
            total = inner_ref[here, :]
            for offset in range(k + 1, reach + 1):
                m = offset - 1 - k
                row = (reach - 1 - m + upper * (2 * m + 1 - reach)) * y_cells
                total = total + scaled[offset] * face_ref[b, pl.ds(pl.multiple_of(row, 8), y_cells), :]
            acc_ref[here, :] = total


def y_border_kernel(x_cells, y_cells, cross_ref, mate_ref, matrix_ref, inner_ref, acc_ref):
    copy_rows(inner_ref, acc_ref)
    odd = lax.axis_index("dy") % 2
    for face_ref, upper in ((mate_ref, 0), (cross_ref, 1)):
        matrix = matrix_ref[upper]
        for first in range(0, face_ref.shape[1], 8):
            block = jnp.concatenate([face_ref[i, pl.ds(first, 8), :] for i in range(reach)], axis=0)
            coarse = block.astype(jnp.bfloat16)
            fine = (block - coarse.astype(jnp.float32)).astype(jnp.bfloat16)
            added = jnp.dot(
                matrix, jnp.concatenate([coarse, fine, coarse], axis=0), preferred_element_type=jnp.float32
            )
            for line in range(8):
                row = (first + line) * y_cells + upper * (y_cells - 8)
                here = pl.ds(pl.multiple_of(row, 8), 8)
                acc_ref[here, :] = inner_ref[here, :] + added[8 * line : 8 * line + 8]


def final_kernel(
    x_cells, y_cells, orb_ref, acc_ref, mine_ref, theirs_ref, late_mine_ref, came_ref, out_ref, held_ref, sems
):
    z_cells = orb_ref.shape[1]
    bands = orb_ref.shape[0] // (x_cells * y_cells)
    own = own_lanes((y_cells, z_cells))
    half, part, late = x_cells // 2, x_cells // 4, came_ref.shape[0]
    copies = []
    for x in range(half):
        if x < late:
            mine, came = late_mine_ref[x], came_ref[x]
        else:
            mine, came = mine_ref[x - late], theirs_ref[x - late]
        near = jnp.where(own, mine, came)
        far = pltpu.roll(jnp.where(own, came, mine), z_cells // 2, 1)
        for t, potential in ((x, near), (x + half, far)):
            for b in range(bands):
                here = pl.ds((b * x_cells + t) * y_cells, y_cells)
                held_ref[here, :] = acc_ref[here, :] + potential * orb_ref[here, :]
        if x % part == part - 1:
            for first in (x + 1 - part, x + 1 - part + half):
                for b in range(bands):
                    piece = pl.ds((b * x_cells + first) * y_cells, part * y_cells)
                    copy = pltpu.make_async_copy(
                        held_ref.at[piece, :], out_ref.at[piece, :], sems.at[len(copies)]
                    )
                    copy.start()
                    copies.append(copy)
    for copy in copies:
        copy.wait()


def whole_kernel(orb_ref, acc_ref, potential_ref, out_ref):
    planes, y_cells, _ = potential_ref.shape
    for line in range(orb_ref.shape[0] // y_cells):
        here = pl.ds(line * y_cells, y_cells)
        out_ref[here, :] = acc_ref[here, :] + potential_ref[line % planes] * orb_ref[here, :]


def band_matrix(size, extent, periodic):
    matrix = np.zeros((size, size), np.float32)
    for i in range(size):
        group = i // extent * extent
        for offset in range(-reach, reach + 1):
            j = i - group + offset
            if periodic:
                j %= extent
            if 0 <= j < extent:
                matrix[i, group + j] += scaled[abs(offset)]
    return matrix


def face_matrix(upper):
    matrix = np.zeros((8, 8, reach, 8), np.float32)
    for k in range(reach):
        for offset in range(k + 1, reach + 1):
            m = offset - 1 - k
            line, source = (7 - k, m) if upper else (k, reach - 1 - m)
            for plane in range(8):
                matrix[plane, line, source, plane] = scaled[offset]
    return matrix.reshape(64, 8 * reach)


def split_constant(matrix):
    coarse = matrix.astype(jnp.bfloat16)
    return coarse, (matrix - coarse.astype(np.float32)).astype(jnp.bfloat16)


def call(kernel, outs, args, spaces=None, out_spaces=None, scratch=(), flops=1 << 20, aliases=None):
    shapes = [jax.ShapeDtypeStruct(shape, jnp.float32) for shape in outs]
    spaces = spaces or [pltpu.VMEM] * len(args)
    out_spaces = out_spaces or [pltpu.VMEM] * len(outs)
    return pl.pallas_call(
        kernel,
        out_shape=shapes,
        in_specs=[pl.BlockSpec(memory_space=space) for space in spaces],
        out_specs=[pl.BlockSpec(memory_space=space) for space in out_spaces],
        scratch_shapes=list(scratch),
        input_output_aliases=aliases or {},
        cost_estimate=pl.CostEstimate(flops=flops, bytes_accessed=0, transcendentals=0),
        compiler_params=pltpu.CompilerParams(vmem_limit_bytes=16 << 20),
    )(*args)


def on_device(orbitals, occupations, core_density, external):
    bands, x_cells, y_cells, z_cells = orbitals.shape
    rows = bands * x_cells * y_cells
    orb = pltpu.with_memory_space_constraint(orbitals.reshape(rows, z_cells), pltpu.HBM)
    flat = (rows, z_cells)
    y_halo = (reach, bands * x_cells, z_cells)
    x_halo = (bands, reach * y_cells, z_cells)
    bind = lambda kernel: functools.partial(kernel, x_cells, y_cells)
    paired = lax.axis_size("band") == 2
    if paired:
        half = x_cells // 2
        shared = half * 3 // 16
        late = half - shared
        planes = lambda count: (count, y_cells, z_cells)
        orb, keep, send, extra = call(
            bind(density_kernel),
            [flat, planes(half), planes(late), planes(shared)],
            [pltpu.with_memory_space_constraint(occupations, pltpu.HBM), orb],
            spaces=[pltpu.HBM, pltpu.HBM],
            scratch=[
                pltpu.SMEM(occupations.shape, jnp.float32),
                pltpu.SemaphoreType.DMA,
                pltpu.SemaphoreType.DMA((8 * bands,)),
            ],
        )
        came = exchanged(send, "band", 0)
    y_mate, y_cross, mate, cross = call(
        bind(halo_kernel), [y_halo, y_halo, x_halo, x_halo], [orb]
    )
    y_mate, y_cross = shifted(y_mate, "dy", True), shifted(y_cross, "dy", False)
    cross = exchanged(cross, "dx", 1)
    if paired:
        dens, extp, parcel = call(
            base_kernel,
            [planes(half), planes(half), planes(3 * shared)],
            [keep, extra, core_density, external],
        )
        parcel = exchanged(parcel, "band", 0)
        (late_mine,) = call(potential_kernel, [planes(late)], [dens, extp, came])
        came = exchanged(late_mine, "band", 0)
        orb, late_mine = lax.optimization_barrier((orb, late_mine))
    else:
        own_density = jnp.sum(occupations[:, None, None, None] * orbitals * orbitals, axis=0)
        total = lax.psum_scatter(own_density, "band", scatter_dimension=2, tiled=True)
        owned = external - slater * (total + core_density) ** (1.0 / 3.0)
        potential = lax.all_gather(owned, "band", axis=2, tiled=True)
    tile = 8 * y_cells
    middle = np.float32(scaled[0]) * np.eye(tile, dtype=np.float32)
    coarse, fine = split_constant(band_matrix(tile, y_cells, False) + middle)
    ymat = np.concatenate([coarse, fine], axis=0)
    coarse, fine = split_constant(band_matrix(z_cells, z_cells, True))
    zmat = np.block([[coarse, fine], [coarse, np.zeros_like(fine)]])
    (acc,) = call(
        bind(stencil_kernel), [flat], [orb, jnp.asarray(ymat), jnp.asarray(zmat)], flops=1 << 28
    )
    acc, mate = lax.optimization_barrier((acc, mate))
    mate = exchanged(mate, "dx", 0)
    if paired:
        acc, dens = lax.optimization_barrier((acc, dens))
        mine, theirs, owned = call(
            owned_kernel,
            [planes(shared), planes(shared), core_density.shape],
            [dens, extp, extra, parcel, late_mine],
        )
        acc, owned = lax.optimization_barrier((acc, owned))
    border = lambda which: functools.partial(x_border_kernel, x_cells, y_cells, which)
    sides = []
    for upper in (False, True):
        coarse, fine = split_constant(face_matrix(upper))
        sides.append(np.concatenate([coarse, coarse, fine], axis=1))
    (acc,) = call(
        bind(y_border_kernel), [flat], [y_cross, y_mate, jnp.asarray(np.stack(sides)), acc], flops=FY
    )
    (acc,) = call(border(False), [flat], [acc, cross], flops=FX)
    (acc,) = call(border(True), [flat], [acc, mate], flops=FM)
    if paired:
        (applied,) = call(
            bind(final_kernel),
            [flat],
            [orb, acc, mine, theirs, late_mine, came],
            out_spaces=[pltpu.HBM],
            scratch=[pltpu.VMEM(flat, jnp.float32), pltpu.SemaphoreType.DMA((8 * bands,))],
        )
    else:
        (applied,) = call(whole_kernel, [flat], [orb, acc, potential])
    return applied.reshape(orbitals.shape), owned


def solution(mesh):
    return jax.shard_map(
        on_device,
        mesh=mesh,
        in_specs=(
            P("band", "dx", "dy", None),
            P("band"),
            P("dx", "dy", "band"),
            P("dx", "dy", "band"),
        ),
        out_specs=(P("band", "dx", "dy", None), P("dx", "dy", "band")),
        check_vma=False,
    )
```
